32 devices in a mesh: cube: 16 (over z, y, x), cores: 2 (over core).
Axes of the slice: x: 2, y: 2, z: 4, core: 2. Of those that a mesh axis runs over, the one named last changes fastest.
Arguments:
- rhs: float32 [4, 8192, 256], P(None, ('cube', 'cores')), may hold values from -6 to 6
- dinv: float32 [4, 8192, 512], P(None, ('cube', 'cores')), may hold values from -1 to 2.5, as said below
- own_update: float32 [4, 8192, 512], P(None, ('cube', 'cores')), may hold values from -0.125 to 0.125
- partner_update: float32 [4, 8192, 512], P(None, ('cube', 'cores')), may hold values from -0.125 to 0.125
- cot_solved: float32 [4, 8192, 256], P(None, ('cube', 'cores')), may hold values from -6 to 6
- cot_top: float32 [8192, 256], P(('cube', 'cores')), may hold values from -6 to 6
- elem_map: int32 [16, 512], P('cube'), may hold values from 0 to 511, each once within a row
Outputs:
- solved: float32 [4, 8192, 256], P(None, ('cube', 'cores'))
- top_update: float32 [8192, 256], P(('cube', 'cores'))
- grad_rhs: float32 [4, 8192, 256], P(None, ('cube', 'cores'))
- element_grad: float32 [4, 512, 8192], P(None, 'cube', 'cores')
The draws below stay inside these ranges and needn't reach their ends.
Inputs may be any that keep to these rules, and one draw needn't show every extreme that they name: Each row of elem_map is a permutation of 0 .. 511. Each block of dinv is the inverse of a well conditioned diagonal block.
All inputs are finite; a program needn't handle non-finite values.
Results may differ from the reference program's by a relative error of at most 0.00012.
Values sent between devices are 32-bit elements; how exact they have to be, the bound alone decides.
No kernel may reach another device: no remote copies, remote signals or barrier semaphores. Data moves between devices by JAX's collectives and lax.ppermute only.
A program may use at most 64 MiB of HBM per device.

```python
import jax
import jax.numpy as jnp
from jax import lax

R = 512
K = 256
LEVELS = 4
NR = 8192
N_CUBE = 16
N_CORES = 2


def draw_dinv(key, part):
    first, second = jax.random.split(jax.random.fold_in(key, 17))
    rows = jnp.arange(NR, dtype=jnp.int32) % R
    cols = jnp.arange(R, dtype=jnp.int32)
    ident = (rows[:, None] == cols[None, :]).astype(jnp.float32)
    scale_off = 1.0 / jnp.sqrt(jnp.float32(R))
    off = jnp.clip(jax.random.normal(first, (LEVELS, NR, R), jnp.float32), -4.0, 4.0) * (0.5 * scale_off)
    diag = jax.random.uniform(second, (LEVELS, NR, 1), jnp.float32, 0.8, 1.6)
    return diag * ident + off * (1.0 - ident)


def steps_of(stream_key, extent, cuts, least, largest):
    loudness, own = 1.0, jax.random.fold_in(stream_key, 6)
    for position, blocks in cuts:
        draws = jnp.exp(jax.random.uniform(jax.random.fold_in(own, position), (blocks,), jnp.float32, least / len(cuts), largest / len(cuts)))
        loudness = loudness * jnp.repeat(draws, extent[position] // blocks).reshape([-1 if axis == position else 1 for axis in range(len(extent))])
    return loudness


def normal_values(key, shape, spread, reach, cuts=(), kind=jnp.bfloat16):
    entries = spread * jax.random.normal(key, shape, jnp.float32)
    if cuts:
        entries = entries * steps_of(key, shape, cuts, -0.22, 0.18)
    return jnp.clip(entries, -reach, reach).astype(kind)


def setup_inputs(seed: int = 0) -> dict:
    key_of = jax.random.split(jax.random.key(seed), 8)
    return {
        "rhs": normal_values(key_of[0], (LEVELS, NR, K), 1.0, 6.0, ((1, 32),), jnp.float32),
        "dinv": draw_dinv(jax.random.fold_in(key_of[7], 71), 0),
        "own_update": normal_values(key_of[2], (LEVELS, NR, R), (4 * R) ** -0.5, 0.125, ((1, 32),), jnp.float32),
        "partner_update": normal_values(key_of[3], (LEVELS, NR, R), (4 * R) ** -0.5, 0.125, ((1, 32),), jnp.float32),
        "cot_solved": normal_values(key_of[4], (LEVELS, NR, K), 1.0, 6.0, ((1, 32),), jnp.float32),
        "cot_top": normal_values(key_of[5], (NR, K), 1.0, 6.0, ((0, 32),), jnp.float32),
        "elem_map": jax.vmap(lambda own: jax.random.permutation(own, R))(jax.random.split(key_of[6], N_CUBE)).reshape((N_CUBE, R)).astype(jnp.int32),
    }


def blockmul(mat, vec):
    return jnp.einsum("pij,pjk->pik", mat, vec, precision=lax.Precision.HIGHEST)


def blockmul_t(mat, vec):
    return jnp.einsum("pji,pjk->pik", mat, vec, precision=lax.Precision.HIGHEST)


def reference(rhs, dinv, own_update, partner_update, cot_solved, cot_top, elem_map):
    parts = N_CUBE
    half = R // N_CORES
    logp = N_CUBE.bit_length() - 1
    owners = jnp.arange(parts, dtype=jnp.int32)
    update = jnp.zeros((parts, R, K), jnp.float32)
    solved_list = []
    for level in range(LEVELS):
        bit = logp - LEVELS + level
        partner = owners ^ (1 << bit)
        dmat = dinv[level].reshape(parts, R, R)
        solved_now = blockmul(dmat, rhs[level].reshape(parts, R, K) - update)
        solved_list.append(solved_now)
        update = blockmul(own_update[level].reshape(parts, R, R), solved_now) + blockmul(partner_update[level].reshape(parts, R, R), solved_now[partner])
    top_update = update.reshape(NR, K)
    backward = cot_top.reshape(parts, R, K)
    grads = [None] * LEVELS
    blocks = [None] * LEVELS
    for level in reversed(range(LEVELS)):
        bit = logp - LEVELS + level
        partner = owners ^ (1 << bit)
        pmat = partner_update[level].reshape(parts, R, R)
        ybar = cot_solved[level].reshape(parts, R, K) + blockmul_t(own_update[level].reshape(parts, R, R), backward) + blockmul_t(pmat[partner], backward[partner])
        outer_t = jnp.einsum("pjk,pik->pji", solved_list[level], backward, precision=lax.Precision.HIGHEST)
        placed = jnp.zeros((parts, R, R), jnp.float32).at[owners[:, None], elem_map].set(outer_t)
        placed = placed.reshape(parts, R, N_CORES, half).transpose(1, 2, 0, 3).reshape(R, NR)
        blocks[level] = placed
        gnow = blockmul_t(dinv[level].reshape(parts, R, R), ybar)
        grads[level] = gnow.reshape(NR, K)
        backward = -gnow
    solved = jnp.stack([s.reshape(NR, K) for s in solved_list])
    return solved, top_update, jnp.stack(grads), jnp.stack(blocks)
```

```python
import functools

import jax
import jax.numpy as jnp
from jax import lax
from jax.experimental import pallas as pl
from jax.experimental.pallas import tpu as pltpu
from jax.sharding import PartitionSpec as P

F32, BF16 = jnp.float32, jnp.bfloat16
VMEM = pltpu.VMEM


def partner(x, distance):
    return lax.ppermute(x, "cube", [(i, i ^ 1 << distance) for i in range(lax.axis_size("cube"))])


def swap(x):
    return lax.ppermute(x, "cores", [(0, 1), (1, 0)])


def split(x):
    hi = x.astype(BF16)
    return hi, (x - hi.astype(F32)).astype(BF16)


def dot(a, b):
    return lax.dot_general(a, b, (((1,), (0,)), ((), ())), preferred_element_type=F32)


def mul(hi, lo, v):
    n = v.shape[1]
    vh, vl = split(v)
    t = dot(hi, jnp.concatenate([vh, vl], axis=1))
    return t[:, :n] + t[:, n:] + dot(lo, vh)


def mul_t(v, hi, lo):
    n = v.shape[0]
    vh, vl = split(v)
    t = dot(jnp.concatenate([vh, vl], axis=0), hi)
    return t[:n] + t[n:] + dot(vh, lo)


def call(kernel, args, outs, scratch=(), levels=None, flops=0, limit=12):
    specs, ops = [], []
    for a in args:
        if isinstance(a, tuple):
            arr, level = a
            specs.append(
                pl.BlockSpec((None, *arr.shape[1:]), functools.partial(lambda k, i: (k, 0, 0), level))
            )
        elif a.dtype == jnp.int32 and a.shape == (1,):
            arr = a
            specs.append(pl.BlockSpec(memory_space=pltpu.SMEM))
        else:
            arr = a
            specs.append(pl.BlockSpec(arr.shape, functools.partial(lambda r, i: (0,) * r, arr.ndim)))
        ops.append(arr)
    nbytes = sum(4 * s.size for s in outs)
    return pl.pallas_call(
        kernel,
        grid=(1,),
        out_shape=tuple(outs),
        in_specs=specs,
        out_specs=tuple(
            pl.BlockSpec(s.shape, functools.partial(lambda r, i: (0,) * r, len(s.shape))) for s in outs
        ),
        scratch_shapes=list(scratch),
        compiler_params=pltpu.CompilerParams(vmem_limit_bytes=limit << 20),
        cost_estimate=pl.CostEstimate(flops=flops, bytes_accessed=nbytes, transcendentals=0),
    )(*ops)


def shape(*s, dtype=F32):
    return jax.ShapeDtypeStruct(s, dtype)


def halves(c, h):
    mine = pl.multiple_of(c * h, h)
    theirs = pl.multiple_of((1 - c) * h, h)
    return mine, theirs


def prep_kernel(c_ref, m_ref, t_ref, hi_ref, lo_ref):
    h = m_ref.shape[0]
    for ref, off in zip((m_ref, t_ref), halves(c_ref[0], h)):
        hi, lo = split(ref[...])
        hi_ref[pl.ds(off, h), :] = hi
        lo_ref[pl.ds(off, h), :] = lo


def own_cols(c, m_ref, t_ref, dst):
    h, k = m_ref.shape[0], m_ref.shape[1] // 2
    cols = pl.ds(pl.multiple_of(c * k, k), k)
    for ref, off in zip((m_ref, t_ref), halves(c, h)):
        dst[pl.ds(off, h), :] = ref[:, cols]


def own_cols_t(c, m_ref, t_ref, dst):
    h, k = m_ref.shape[0], m_ref.shape[1] // 2
    cols = pl.ds(pl.multiple_of(c * k, k), k)
    for ref, off in zip((m_ref, t_ref), halves(c, h)):
        dst[:, pl.ds(off, h)] = ref[:, cols].T


def fwd_first(c_ref, rm_ref, rt_ref, dh, dl, s_ref, r_ref):
    own_cols(c_ref[0], rm_ref, rt_ref, r_ref)
    s_ref[...] = mul(dh[...], dl[...], r_ref[...])


def fwd_own(s_ref, oh, ol, a_ref):
    a_ref[...] = mul(oh[...], ol[...], s_ref[...])


def fwd_next(c_ref, a_ref, sp_ref, ph, plo, rm_ref, rt_ref, dh, dl, s_ref, r_ref):
    own_cols(c_ref[0], rm_ref, rt_ref, r_ref)
    u = a_ref[...] + mul(ph[...], plo[...], sp_ref[...])
    s_ref[...] = mul(dh[...], dl[...], r_ref[...] - u)


def fwd_last(c_ref, a_ref, sp_ref, ph, plo, keep_ref, send_ref, u_ref):
    u_ref[...] = a_ref[...] + mul(ph[...], plo[...], sp_ref[...])
    h = keep_ref.shape[0]
    mine, theirs = halves(c_ref[0], h)
    keep_ref[...] = u_ref[pl.ds(mine, h), :]
    send_ref[...] = u_ref[pl.ds(theirs, h), :]


def bwd_first(c_ref, tm_ref, tt_ref, ph, plo, y_ref, w_ref, wm_ref, wt_ref):
    c = c_ref[0]
    own_cols_t(c, tm_ref, tt_ref, w_ref)
    y_ref[...] = mul_t(w_ref[...], ph[...], plo[...])
    k = w_ref.shape[0]
    mine, theirs = halves(c, k)
    wm_ref[...] = tm_ref[:, pl.ds(mine, k)].T
    wt_ref[...] = tm_ref[:, pl.ds(theirs, k)].T


def bwd_own(c_ref, w_ref, oh, ol, cm_ref, ct_ref, b_ref):
    own_cols_t(c_ref[0], cm_ref, ct_ref, b_ref)
    b_ref[...] += mul_t(w_ref[...], oh[...], ol[...])


def bwd_next(c_ref, b_ref, y_in, dh, dl, ph, plo, y_ref, w_ref, wm_ref, ws_ref):
    w_ref[...] = -mul_t(b_ref[...] + y_in[...], dh[...], dl[...])
    y_ref[...] = mul_t(w_ref[...], ph[...], plo[...])
    h = wm_ref.shape[1]
    mine, theirs = halves(c_ref[0], h)
    wm_ref[...] = w_ref[:, pl.ds(mine, h)]
    ws_ref[...] = w_ref[:, pl.ds(theirs, h)]


def bwd_last(c_ref, b_ref, y_in, dh, dl, wm_ref, ws_ref, w_ref):
    w_ref[...] = -mul_t(b_ref[...] + y_in[...], dh[...], dl[...])
    h = wm_ref.shape[1]
    mine, theirs = halves(c_ref[0], h)
    wm_ref[...] = w_ref[:, pl.ds(mine, h)]
    ws_ref[...] = w_ref[:, pl.ds(theirs, h)]


def outer_kernel(c_ref, s_ref, st_ref, wm_ref, wt_ref, map_ref, o_ref, solved_ref):
    c = c_ref[0]
    r, k = s_ref.shape
    h = r // 2
    mine, _ = halves(c, h)
    km, kt = halves(c, k)
    solved_ref[:, pl.ds(km, k)] = s_ref[pl.ds(mine, h), :]
    solved_ref[:, pl.ds(kt, k)] = st_ref[pl.ds(mine, h), :]
    pick = jnp.where(lax.broadcasted_iota(jnp.int32, (r, r), 0) == map_ref[...], 1.0, 0.0).astype(BF16)
    sh, sl = split(jnp.concatenate([s_ref[...], st_ref[...]], axis=1))
    ph = dot(pick, sh).astype(BF16)
    plo = dot(pick, sl).astype(BF16)
    wh, wl = split(jnp.concatenate([wm_ref[...], wt_ref[...]], axis=0))
    o = dot(ph, wh) + dot(ph, wl) + dot(plo, wh)
    o_ref[...] = o.reshape(o_ref.shape)


def grad_kernel(c_ref, wm_ref, wt_ref, g_ref):
    k = wm_ref.shape[0]
    km, kt = halves(c_ref[0], k)
    g_ref[:, pl.ds(km, k)] = -wm_ref[...].T
    g_ref[:, pl.ds(kt, k)] = -wt_ref[...].T


def join_kernel(c_ref, m_ref, t_ref, o_ref):
    k = m_ref.shape[1]
    km, kt = halves(c_ref[0], k)
    o_ref[:, pl.ds(km, k)] = m_ref[...]
    o_ref[:, pl.ds(kt, k)] = t_ref[...]


def local(rhs, dinv, own, far, cot, top, elem_map):
    levels, h, k = rhs.shape
    r, kh = 2 * h, k // 2
    n = lax.axis_size("cube")
    base = n.bit_length() - 1 - levels
    c = lax.axis_index("cores").astype(jnp.int32).reshape(1)
    fl = 3 * 2 * r * r * kh

    far_t, top_t = swap(far), swap(top)
    dinv_t, rhs_t = swap(dinv), swap(rhs)
    own_t, cot_t = swap(own), swap(cot)

    def prep(mine, theirs, level):
        return call(
            prep_kernel, [c, (mine, level), (theirs, level)], [shape(r, r, dtype=BF16)] * 2, flops=r * r
        )

    top_level = levels - 1
    pm, dm, om = [None] * levels, [None] * levels, [None] * levels
    for t in range(levels):
        pm[top_level - t] = prep(far, far_t, top_level - t)
        dm[t] = prep(dinv, dinv_t, t)
        om[t] = prep(own, own_t, t)

    vec, vec_t = shape(r, kh), shape(kh, r)
    s, w, wm, wt = [None] * levels, [None] * levels, [None] * levels, [None] * levels
    y, w_full, wm[top_level], wt[top_level] = call(
        bwd_first, [c, top, top_t, *pm[top_level]], [vec_t, vec_t, shape(kh, h), shape(kh, h)], flops=fl
    )
    s[0], = call(fwd_first, [c, (rhs, 0), (rhs_t, 0), *dm[0]], [vec], [VMEM((r, kh), F32)], flops=fl)
    blocks, solved, grads = [None] * levels, [None] * levels, [None] * levels
    top_update = None
    for t in range(levels):
        lf, lb = t, top_level - t
        yp = partner(y, base + lb)
        sp = partner(s[lf], base + lf)
        a, = call(fwd_own, [s[lf], *om[lf]], [vec], flops=fl)
        b, = call(bwd_own, [c, w_full, *om[lb], (cot, lb), (cot_t, lb)], [vec_t], flops=fl)
        if t < top_level:
            s[lf + 1], = call(
                fwd_next,
                [c, a, sp, *pm[lf], (rhs, lf + 1), (rhs_t, lf + 1), *dm[lf + 1]],
                [vec],
                [VMEM((r, kh), F32)],
                flops=2 * fl,
            )
            y, w_full, wm[lb - 1], ws = call(
                bwd_next,
                [c, b, yp, *dm[lb], *pm[lb - 1]],
                [vec_t, vec_t, shape(kh, h), shape(kh, h)],
                flops=2 * fl,
            )
            wt[lb - 1] = swap(ws)
        else:
            keep, send = call(
                fwd_last, [c, a, sp, *pm[lf]], [shape(h, kh)] * 2, [VMEM((r, kh), F32)], flops=fl
            )
            top_update, = call(join_kernel, [c, keep, swap(send)], [shape(h, k)])
            gm, gs = call(
                bwd_last, [c, b, yp, *dm[0]], [shape(kh, h)] * 2, [VMEM((kh, r), F32)], flops=fl
            )
            grads[0], = call(grad_kernel, [c, gm, swap(gs)], [shape(h, k)])
    st = [swap(x) for x in s]
    for level in (2, 1, 3, 0) if levels == 4 else range(levels):
        o, solved[level] = call(
            outer_kernel,
            [c, s[level], st[level], wm[level], wt[level], elem_map],
            [shape(n, r // n, h), shape(h, k)],
            flops=2 * r * r * k * 2 + 6 * r * k * h,
        )
        blocks[level] = lax.all_to_all(o, "cube", split_axis=0, concat_axis=0, tiled=True)
        if level < top_level:
            grads[level + 1], = call(grad_kernel, [c, wm[level], wt[level]], [shape(h, k)])
    element_grad = jnp.stack([x.transpose(1, 0, 2).reshape(r // n, n * h) for x in blocks])
    return jnp.stack(solved), top_update, jnp.stack(grads), element_grad


def solution(mesh):
    rows = P(None, ("cube", "cores"), None)
    return jax.shard_map(
        local,
        mesh=mesh,
        in_specs=(rows, rows, rows, rows, rows, P(("cube", "cores"), None), P("cube", None)),
        out_specs=(rows, P(("cube", "cores"), None), rows, P(None, "cube", "cores")),
        check_vma=False,
    )
```

```python
import functools
import types

import jax
import jax.numpy as jnp
from jax import lax
from jax.experimental import pallas as pl
from jax.experimental.pallas import tpu as pltpu
from jax.sharding import PartitionSpec as P

F32, BF16 = jnp.float32, jnp.bfloat16
VMEM = pltpu.VMEM
NEAR = 4


def partner(x, distance):
    return lax.ppermute(x, "cube", [(i, i ^ 1 << distance) for i in range(lax.axis_size("cube"))])


def swap(x):
    return lax.ppermute(x, "cores", [(0, 1), (1, 0)])


def split(x):
    hi = x.astype(BF16)
    return hi, (x - hi.astype(F32)).astype(BF16)


def dot(a, b):
    return lax.dot_general(a, b, (((1,), (0,)), ((), ())), preferred_element_type=F32)


def mul(hi, lo, v):
    n = v.shape[1]
    vh, vl = split(v)
    t = dot(hi, jnp.concatenate([vh, vl], axis=1))
    return t[:, :n] + t[:, n:] + dot(lo, vh)


def mul_t(v, hi, lo):
    n = v.shape[0]
    vh, vl = split(v)
    t = dot(jnp.concatenate([vh, vl], axis=0), hi)
    return t[:n] + t[n:] + dot(vh, lo)


class Sequence:
    def __init__(self):
        self.last = None

    def __call__(self, kernel, args, outs, scratch=(), limit=8, hbm=()):
        args = list(args)
        if self.last is not None:
            args[0] = after(args[0], self.last)
        for i in hbm:
            args[i] = pltpu.with_memory_space_constraint(args[i], pltpu.HBM)
        res = pl.pallas_call(
            kernel,
            out_shape=tuple(outs),
            in_specs=[pl.BlockSpec(memory_space=pltpu.HBM if i in hbm else VMEM) for i in range(len(args))],
            out_specs=tuple(pl.BlockSpec(memory_space=VMEM) for _ in outs),
            scratch_shapes=list(scratch),
            compiler_params=pltpu.CompilerParams(vmem_limit_bytes=limit << 20),
        )(*args)
        self.last = res[0]
        return res

    def named(self, kernel, args, outs, **more):
        def body(*refs):
            ins, rest = refs[: len(args)], refs[len(args) :]
            kernel(
                types.SimpleNamespace(**dict(zip(args, ins))),
                types.SimpleNamespace(**dict(zip(outs, rest))),
                *rest[len(outs) :],
            )

        return dict(zip(outs, self(body, args.values(), outs.values(), **more)))


def shape(*s, dtype=F32):
    return jax.ShapeDtypeStruct(s, dtype)


def after(x, *others):
    return lax.optimization_barrier((x, *others))[0]


def halves(h):
    c = lax.axis_index("cores")
    return pl.multiple_of(c * h, h), pl.multiple_of((1 - c) * h, h)


def whole(m_ref, t_ref, level, hi_ref, lo_ref):
    h = hi_ref.shape[0] // 2
    for ref, off in zip((m_ref, t_ref), halves(h)):
        hi, lo = split(ref[...] if level is None else ref[level])
        hi_ref[pl.ds(off, h), :] = hi
        lo_ref[pl.ds(off, h), :] = lo


def take_kernel(last, far_ref, dinv_ref, pf_ref, d0_ref, sem):
    copies = [
        pltpu.make_async_copy(far_ref.at[last], pf_ref, sem.at[0]),
        pltpu.make_async_copy(dinv_ref.at[0], d0_ref, sem.at[1]),
    ]
    for copy in copies:
        copy.start()
    for copy in copies:
        copy.wait()


def first_kernel(refs, outs):
    h, k = refs.top.shape[0], refs.top.shape[1] // 2
    mine, theirs = halves(k)
    row_mine, row_theirs = halves(h)
    whole(refs.pf, refs.pf_t, None, outs.ph, outs.pl)
    outs.wm[...] = refs.top[:, pl.ds(mine, k)].T
    outs.w[:, pl.ds(row_mine, h)] = outs.wm[...]
    outs.w[:, pl.ds(row_theirs, h)] = refs.top_t[:, pl.ds(mine, k)].T
    outs.y[...] = mul_t(outs.w[...], outs.ph[...], outs.pl[...])
    whole(refs.d0, refs.d0_t, None, outs.dh, outs.dl)
    for level in range(refs.rhs.shape[0]):
        outs.rows[level, pl.ds(row_mine, h), :] = refs.rhs[level, :, pl.ds(mine, k)]
        outs.rows[level, pl.ds(row_theirs, h), :] = refs.rhs_t[level, :, pl.ds(mine, k)]
    outs.s[...] = mul(outs.dh[...], outs.dl[...], outs.rows[0])
    outs.wt[...] = refs.top[:, pl.ds(theirs, k)].T


def prep_kernel(new, refs, outs, buf, sem):
    copies = [
        pltpu.make_async_copy(getattr(refs, name).at[level], buf.at[i], sem.at[i])
        for i, (name, level) in enumerate(new)
    ]
    for copy in copies:
        copy.start()
    for i, (name, level) in enumerate(new):
        copies[i].wait()
        hi, lo = getattr(outs, f"{name}{level}h"), getattr(outs, f"{name}{level}l")
        h = hi.shape[0] // 2
        mine, theirs = halves(h)
        for v, off in ((buf[i], mine), (getattr(refs, name + "_t")[level], theirs)):
            v_hi, v_lo = split(v)
            hi[pl.ds(off, h), :] = v_hi
            lo[pl.ds(off, h), :] = v_lo


def own_kernel(lb, refs, outs):
    outs.a[...] = mul(refs.ph[...], refs.pl[...], refs.s[...])
    h, k = refs.cot.shape[1], refs.cot.shape[2] // 2
    mine, _ = halves(k)
    for ref, off in zip((refs.cot, refs.cot_t), halves(h)):
        outs.b[:, pl.ds(off, h)] = ref[lb, :, pl.ds(mine, k)].T
    outs.b[...] += mul_t(refs.w[...], refs.qh[...], refs.ql[...])


def fwd_next(level, refs, outs):
    u = refs.a[...] + mul(refs.ph[...], refs.pl[...], refs.sp[...])
    outs.s[...] = mul(refs.dh[...], refs.dl[...], refs.rows[level] - u)


def bwd_next(refs, outs):
    outs.w[...] = -mul_t(refs.b[...] + refs.yp[...], refs.dh[...], refs.dl[...])
    outs.y[...] = mul_t(outs.w[...], refs.ph[...], refs.pl[...])
    h = outs.wm.shape[1]
    mine, theirs = halves(h)
    outs.wm[...] = outs.w[:, pl.ds(mine, h)]
    outs.ws[...] = outs.w[:, pl.ds(theirs, h)]


def bwd_last(refs, outs):
    w = refs.b[...] + refs.yp[...]
    outs.g[...] = -mul_t(w, refs.dh[...], refs.dl[...])
    h = outs.gm.shape[1]
    mine, theirs = halves(h)
    outs.gm[...] = outs.g[:, pl.ds(mine, h)]
    outs.gs[...] = outs.g[:, pl.ds(theirs, h)]


def fwd_last(refs, outs):
    outs.u[...] = refs.a[...] + mul(refs.ph[...], refs.pl[...], refs.sp[...])
    h = outs.um.shape[0]
    mine, theirs = halves(h)
    outs.um[...] = outs.u[pl.ds(mine, h), :]
    outs.us[...] = outs.u[pl.ds(theirs, h), :]


def outer_kernel(batch, by_near, map_ref, *refs):
    ins, outs = refs[: 4 * batch], refs[4 * batch :]
    r = ins[0].shape[0]
    e = outs[0].shape[2]
    target = map_ref[...] ^ (lax.axis_index("cube") * e)
    pick = jnp.where(lax.broadcasted_iota(jnp.int32, (r, r), 0) == target, 1.0, 0.0).astype(BF16)
    for i in range(batch):
        s_ref, st_ref, wm_ref, wt_ref = ins[4 * i : 4 * i + 4]
        sh, sl = split(jnp.concatenate([s_ref[...], st_ref[...]], axis=1))
        ph = dot(pick, sh).astype(BF16)
        plo = dot(pick, sl).astype(BF16)
        wh, wl = split(jnp.concatenate([wm_ref[...], wt_ref[...]], axis=0))
        o = dot(ph, wh) + dot(ph, wl) + dot(plo, wh)
        for j, out in enumerate(outs):
            for q in range(out.shape[1]):
                at = (j + NEAR * q if by_near else q + NEAR * j) * e
                out[i, q] = o[at : at + e]


def turn_kernel(n_in, *refs):
    ins, outs = refs[:n_in], refs[n_in:]
    for q, out in enumerate(outs):
        for j, ref in enumerate(ins):
            for i in range(ref.shape[0]):
                out[i, j] = ref[i, q]


def results_kernel(*refs):
    solved_ref, grad_ref = refs[-2:]
    levels, h, k = solved_ref.shape
    k //= 2
    mine, _ = halves(h)
    own, other = (pl.ds(x, k) for x in halves(k))
    for level in range(levels):
        s_ref, st_ref, gm_ref, gt_ref = refs[4 * level : 4 * level + 4]
        solved_ref[level, :, own] = s_ref[pl.ds(mine, h), :]
        solved_ref[level, :, other] = st_ref[pl.ds(mine, h), :]
        grad_ref[level, :, own] = -gm_ref[...].T
        grad_ref[level, :, other] = -gt_ref[...].T


def join_kernel(m_ref, t_ref, o_ref):
    k = m_ref.shape[1]
    own, other = (pl.ds(x, k) for x in halves(k))
    o_ref[:, own] = m_ref[...]
    o_ref[:, other] = t_ref[...]


def place_kernel(plan, *refs):
    o_ref, sem = refs[-2:]
    me = lax.axis_index("cube")
    h = refs[0].shape[-1]
    copies = []
    for i, (array, index, level, source) in enumerate(plan):
        col = pl.multiple_of((me ^ source) * h, h)
        copies.append(
            pltpu.make_async_copy(refs[array].at[index], o_ref.at[level, :, pl.ds(col, h)], sem.at[i])
        )
    for copy in copies:
        copy.start()
    for copy in copies:
        copy.wait()


def place(run, blocks, plan, out, so_far=None):
    more = [] if so_far is None else [so_far]
    res = pl.pallas_call(
        functools.partial(place_kernel, plan),
        out_shape=out,
        in_specs=[pl.BlockSpec(memory_space=pl.ANY)] * (len(blocks) + len(more)),
        out_specs=pl.BlockSpec(memory_space=pl.ANY),
        scratch_shapes=[pltpu.SemaphoreType.DMA((len(plan),))],
        input_output_aliases={len(blocks): 0} if more else {},
        compiler_params=pltpu.CompilerParams(vmem_limit_bytes=1 << 20),
    )(after(blocks[0], run.last), *blocks[1:], *more)
    run.last = res
    return res


def local(rhs, dinv, own, far, cot, top, elem_map):
    levels, h, k = rhs.shape
    r, kh = 2 * h, k // 2
    n = lax.axis_size("cube")
    base = n.bit_length() - 1 - levels
    last = levels - 1
    run = Sequence()
    vec, vec_t, half_t, front = shape(r, kh), shape(kh, r), shape(kh, h), shape(r, r, dtype=BF16)

    top_t = swap(top)
    pf, d0 = run(
        functools.partial(take_kernel, last),
        [far, dinv],
        [shape(h, r)] * 2,
        [pltpu.SemaphoreType.DMA((2,))],
        hbm=(0, 1),
    )
    pf_t, d0_t = swap(pf), swap(d0)
    rhs_t, cot_t = swap(rhs), swap(cot)
    x = run.named(
        first_kernel,
        {"pf": pf, "pf_t": pf_t, "d0": d0, "d0_t": d0_t, "top": top, "top_t": top_t, "rhs": rhs, "rhs_t": rhs_t},
        {
            "s": vec, "y": vec_t, "w": vec_t, "wm": half_t, "wt": half_t, "rows": shape(levels, r, kh),
            "ph": front, "pl": front, "dh": front, "dl": front,
        },
    )
    raw = {"far": far, "own": own, "dinv": dinv}
    raw.update({name + "_t": swap(after(v, top_t, pf_t, d0_t, rhs_t, cot_t)) for name, v in raw.items()})
    parts = {f"far{last}h": x["ph"], f"far{last}l": x["pl"], "dinv0h": x["dh"], "dinv0l": x["dl"]}
    rows = x["rows"]
    s, st, wm, wt = ([None] * levels for _ in range(4))
    s[0], w, y, wm[last], wt[last] = x["s"], x["w"], x["y"], x["wm"], x["wt"]
    st[0] = swap(s[0])

    nears, fars = range(NEAR), range(n // NEAR)

    def outer(batch, by_near):
        one = shape(len(batch), len(fars if by_near else nears), r // n, h)
        return run(
            functools.partial(outer_kernel, len(batch), by_near),
            [elem_map, *(v for q in batch for v in (s[q], st[q], wm[q], wt[q]))],
            [one] * len(nears if by_near else fars),
            limit=12,
        )

    def exchange(arrays, step):
        return [
            arrays[0],
            *(lax.ppermute(v, "cube", [(i, i ^ j * step) for i in range(n)]) for j, v in enumerate(arrays) if j),
        ]

    def turn(arrays):
        batch, count, e, width = arrays[0].shape
        return run(
            functools.partial(turn_kernel, len(arrays)), arrays, [shape(batch, len(arrays), e, width)] * count
        )

    early, late = list(range(1, levels - 1)), [0, last]
    for t in range(levels):
        lf, lb = t, last - t
        yp = partner(y, base + lb)
        if t < last:
            sp = partner(s[lf], base + lf)
        if t == 0:
            new = [(name, q) for name in raw if "_t" not in name for q in range(levels)]
            new = [q for q in new if f"{q[0]}{q[1]}h" not in parts]
            parts.update(
                run.named(
                    functools.partial(prep_kernel, new),
                    {"far_t": raw["far_t"], "own_t": raw["own_t"], "dinv_t": raw["dinv_t"],
                     "far": far, "own": own, "dinv": dinv},
                    {f"{name}{level}{e}": front for name, level in new for e in "hl"},
                    scratch=[VMEM((len(new), h, r), F32), pltpu.SemaphoreType.DMA((len(new),))],
                    hbm=(3, 4, 5),
                )
            )
        x = run.named(
            functools.partial(own_kernel, lb),
            {
                "s": s[lf], "w": w, "cot": cot, "cot_t": cot_t,
                "ph": parts[f"own{lf}h"], "pl": parts[f"own{lf}l"],
                "qh": parts[f"own{lb}h"], "ql": parts[f"own{lb}l"],
            },
            {"a": vec, "b": vec_t},
        )
        a, b = x["a"], x["b"]
        if t == levels - 2:
            crossed = exchange(outer(early, False), NEAR)
        if t < last:
            x = run.named(
                bwd_next,
                {
                    "b": b, "yp": yp,
                    **{p + e: parts[f"{q}{e}"] for e in "hl" for p, q in (("d", f"dinv{lb}"), ("p", f"far{lb - 1}"))},
                },
                {"y": vec_t, "w": vec_t, "wm": half_t, "ws": half_t},
            )
            w, y, wm[lb - 1], wt[lb - 1] = x["w"], x["y"], x["wm"], swap(x["ws"])
            x = run.named(
                functools.partial(fwd_next, t + 1),
                {
                    "a": a, "sp": sp, "rows": rows,
                    **{p + e: parts[f"{q}{e}"] for e in "hl" for p, q in (("p", f"far{lf}"), ("d", f"dinv{lf + 1}"))},
                },
                {"s": vec},
            )
            s[t + 1] = x["s"]
            st[t + 1] = swap(s[t + 1])
    late_in = turn(exchange(outer(late, True), 1))
    late_in = exchange(late_in, NEAR)
    g = run.named(
        bwd_last,
        {"b": b, "yp": yp, "dh": parts["dinv0h"], "dl": parts["dinv0l"]},
        {"g": vec_t, "gm": half_t, "gs": half_t},
    )
    gms, gts = [g["gm"], *wm[:last]], [swap(g["gs"]), *wt[:last]]
    early_in = exchange(turn(crossed), 1)
    sp = partner(after(s[last], *crossed), base + last)
    solved, grads = run(
        results_kernel,
        [v for q in range(levels) for v in (s[q], st[q], gms[q], gts[q])],
        [shape(levels, h, k), shape(levels, h, k)],
    )
    out = shape(levels, r // n, n * h)
    plan = [(m, (i, f), lv, m + NEAR * f) for m in nears for f in fars for i, lv in enumerate(early)]
    element_grad = place(run, early_in, plan, out)
    u = run.named(
        fwd_last,
        {"a": a, "sp": sp, "ph": parts[f"far{last}h"], "pl": parts[f"far{last}l"]},
        {"u": vec, "um": shape(h, kh), "us": shape(h, kh)},
    )
    top_update, = run(join_kernel, [u["um"], swap(u["us"])], [shape(h, k)])
    plan = [(f, (i, m), lv, m + NEAR * f) for m in nears for f in fars for i, lv in enumerate(late)]
    element_grad = place(run, late_in, plan, out, element_grad)
    return solved, top_update, grads, element_grad


def solution(mesh):
    rows = P(None, ("cube", "cores"), None)
    return jax.shard_map(
        local,
        mesh=mesh,
        in_specs=(rows, rows, rows, rows, rows, P(("cube", "cores"), None), P("cube", None)),
        out_specs=(rows, P(("cube", "cores"), None), rows, P(None, "cube", "cores")),
        check_vma=False,
    )
```

```python
import functools
import types

import jax
import jax.numpy as jnp
from jax import lax
from jax.experimental import pallas as pl
from jax.experimental.pallas import tpu as pltpu
from jax.sharding import PartitionSpec as P

F32, BF16 = jnp.float32, jnp.bfloat16
VMEM = pltpu.VMEM
NEAR = 4


def partner(x, distance):
    return lax.ppermute(x, "cube", [(i, i ^ 1 << distance) for i in range(lax.axis_size("cube"))])


def swap(x):
    return lax.ppermute(x, "cores", [(0, 1), (1, 0)])


def both(x):
    return lax.all_gather(x, "cores")


def other(ref):
    return ref[1 - lax.axis_index("cores")] if len(ref.shape) == 3 else ref[...]


def split(x):
    hi = x.astype(BF16)
    return hi, (x - hi.astype(F32)).astype(BF16)


def dot(a, b):
    return lax.dot_general(a, b, (((1,), (0,)), ((), ())), preferred_element_type=F32)


def mul(hi, lo, v):
    n = v.shape[1]
    vh, vl = split(v)
    t = dot(hi, jnp.concatenate([vh, vl], axis=1))
    return t[:, :n] + t[:, n:] + dot(lo, vh)


def mul_t(v, hi, lo):
    n = v.shape[0]
    vh, vl = split(v)
    t = dot(jnp.concatenate([vh, vl], axis=0), hi)
    return t[:n] + t[n:] + dot(vh, lo)


class Sequence:
    def __init__(self):
        self.last = None

    def __call__(self, kernel, args, outs, scratch=(), limit=8, hbm=()):
        args = list(args)
        if self.last is not None:
            args[0] = after(args[0], self.last)
        for i in hbm:
            args[i] = pltpu.with_memory_space_constraint(args[i], pltpu.HBM)
        res = pl.pallas_call(
            kernel,
            out_shape=tuple(outs),
            in_specs=[pl.BlockSpec(memory_space=pltpu.HBM if i in hbm else VMEM) for i in range(len(args))],
            out_specs=tuple(pl.BlockSpec(memory_space=VMEM) for _ in outs),
            scratch_shapes=list(scratch),
            compiler_params=pltpu.CompilerParams(vmem_limit_bytes=limit << 20),
        )(*args)
        self.last = res[-1]
        return res

    def named(self, kernel, args, outs, **more):
        def body(*refs):
            ins, rest = refs[: len(args)], refs[len(args) :]
            kernel(
                types.SimpleNamespace(**dict(zip(args, ins))),
                types.SimpleNamespace(**dict(zip(outs, rest))),
                *rest[len(outs) :],
            )

        return dict(zip(outs, self(body, args.values(), outs.values(), **more)))


def shape(*s, dtype=F32):
    return jax.ShapeDtypeStruct(s, dtype)


def after(x, *others):
    return lax.optimization_barrier((x, *others))[0]


def halves(h):
    c = lax.axis_index("cores")
    return pl.multiple_of(c * h, h), pl.multiple_of((1 - c) * h, h)


def whole(m_ref, t_ref, level, hi_ref, lo_ref):
    h = hi_ref.shape[0] // 2
    for ref, off in zip((m_ref, t_ref), halves(h)):
        hi, lo = split(ref[...] if level is None else ref[level])
        hi_ref[pl.ds(off, h), :] = hi
        lo_ref[pl.ds(off, h), :] = lo


def take_kernel(last, far_ref, dinv_ref, pf_ref, d0_ref, sem):
    copies = [
        pltpu.make_async_copy(far_ref.at[last], pf_ref, sem.at[0]),
        pltpu.make_async_copy(dinv_ref.at[0], d0_ref, sem.at[1]),
    ]
    for copy in copies:
        copy.start()
    for copy in copies:
        copy.wait()


def first_kernel(refs, outs):
    h, k = refs.top.shape[0], refs.top.shape[1] // 2
    mine, theirs = halves(k)
    row_mine, row_theirs = halves(h)
    whole(refs.pf, refs.pf_t, None, outs.ph, outs.pl)
    outs.wm[...] = refs.top[:, pl.ds(mine, k)].T
    outs.w[:, pl.ds(row_mine, h)] = outs.wm[...]
    outs.w[:, pl.ds(row_theirs, h)] = refs.top_t[:, pl.ds(mine, k)].T
    outs.y[...] = mul_t(outs.w[...], outs.ph[...], outs.pl[...])
    whole(refs.d0, refs.d0_t, None, outs.dh, outs.dl)
    for level in range(refs.rhs.shape[0]):
        outs.rows[level, pl.ds(row_mine, h), :] = refs.rhs[level, :, pl.ds(mine, k)]
        outs.rows[level, pl.ds(row_theirs, h), :] = refs.rhs_t[level, :, pl.ds(mine, k)]
    outs.s[...] = mul(outs.dh[...], outs.dl[...], outs.rows[0])
    outs.wt[...] = refs.top[:, pl.ds(theirs, k)].T


def prep_kernel(new, refs, outs, buf, sem):
    copies = [
        pltpu.make_async_copy(getattr(refs, name).at[level], buf.at[i], sem.at[i])
        for i, (name, level) in enumerate(new)
    ]
    for copy in copies:
        copy.start()
    for i, (name, level) in enumerate(new):
        copies[i].wait()
        hi, lo = getattr(outs, f"{name}{level}h"), getattr(outs, f"{name}{level}l")
        h = hi.shape[0] // 2
        mine, theirs = halves(h)
        for v, off in ((buf[i], mine), (getattr(refs, name + "_t")[level], theirs)):
            v_hi, v_lo = split(v)
            hi[pl.ds(off, h), :] = v_hi
            lo[pl.ds(off, h), :] = v_lo


def own_kernel(lb, refs, outs):
    outs.a[...] = mul(refs.ph[...], refs.pl[...], refs.s[...])
    h, k = refs.cot.shape[1], refs.cot.shape[2] // 2
    mine, _ = halves(k)
    for ref, off in zip((refs.cot, refs.cot_t), halves(h)):
        outs.b[:, pl.ds(off, h)] = ref[lb, :, pl.ds(mine, k)].T
    outs.b[...] += mul_t(refs.w[...], refs.qh[...], refs.ql[...])


def fwd_next(level, refs, outs):
    u = refs.a[...] + mul(refs.ph[...], refs.pl[...], refs.sp[...])
    outs.s[...] = mul(refs.dh[...], refs.dl[...], refs.rows[level] - u)


def bwd_next(refs, outs):
    outs.w[...] = -mul_t(refs.b[...] + refs.yp[...], refs.dh[...], refs.dl[...])
    outs.y[...] = mul_t(outs.w[...], refs.ph[...], refs.pl[...])
    h = outs.wm.shape[1]
    mine, theirs = halves(h)
    outs.wm[...] = outs.w[:, pl.ds(mine, h)]
    outs.ws[...] = outs.w[:, pl.ds(theirs, h)]


def bwd_last(refs, outs):
    w = refs.b[...] + refs.yp[...]
    outs.g[...] = -mul_t(w, refs.dh[...], refs.dl[...])
    h = outs.gm.shape[1]
    mine, theirs = halves(h)
    outs.gm[...] = outs.g[:, pl.ds(mine, h)]
    outs.gs[...] = outs.g[:, pl.ds(theirs, h)]


def fwd_last(refs, outs):
    outs.u[...] = refs.a[...] + mul(refs.ph[...], refs.pl[...], refs.sp[...])
    h = outs.um.shape[0]
    mine, theirs = halves(h)
    outs.um[...] = outs.u[pl.ds(mine, h), :]
    outs.us[...] = outs.u[pl.ds(theirs, h), :]


def outer_kernel(batch, by_near, map_ref, *refs):
    ins, outs = refs[: 4 * batch], refs[4 * batch :]
    r = ins[0].shape[0]
    e = outs[0].shape[2]
    target = map_ref[...] ^ (lax.axis_index("cube") * e)
    pick = jnp.where(lax.broadcasted_iota(jnp.int32, (r, r), 0) == target, 1.0, 0.0).astype(BF16)
    for i in range(batch):
        s_ref, st_ref, wm_ref, wt_ref = ins[4 * i : 4 * i + 4]
        sh, sl = split(jnp.concatenate([s_ref[...], other(st_ref)], axis=1))
        ph = dot(pick, sh).astype(BF16)
        plo = dot(pick, sl).astype(BF16)
        wh, wl = split(jnp.concatenate([wm_ref[...], other(wt_ref)], axis=0))
        o = dot(ph, wh) + dot(ph, wl) + dot(plo, wh)
        for j, out in enumerate(outs):
            for q in range(out.shape[1]):
                at = (j + NEAR * q if by_near else q + NEAR * j) * e
                out[i, q] = o[at : at + e]


def turn_kernel(n_in, *refs):
    ins, outs = refs[:n_in], refs[n_in:]
    for q, out in enumerate(outs):
        for j, ref in enumerate(ins):
            for i in range(ref.shape[0]):
                out[i, j] = ref[i, q]


def results_kernel(*refs):
    solved_ref, grad_ref = refs[-2:]
    levels, h, k = solved_ref.shape
    k //= 2
    mine, _ = halves(h)
    own, theirs = (pl.ds(x, k) for x in halves(k))
    for level in range(levels):
        s_ref, st_ref, gm_ref, gt_ref = refs[4 * level : 4 * level + 4]
        solved_ref[level, :, own] = s_ref[pl.ds(mine, h), :]
        st = st_ref if len(st_ref.shape) == 2 else st_ref.at[1 - lax.axis_index("cores")]
        solved_ref[level, :, theirs] = st[pl.ds(mine, h), :]
        grad_ref[level, :, own] = -gm_ref[...].T
        grad_ref[level, :, theirs] = -other(gt_ref).T


def join_kernel(m_ref, t_ref, o_ref):
    k = m_ref.shape[1]
    own, theirs = (pl.ds(x, k) for x in halves(k))
    o_ref[:, own] = m_ref[...]
    o_ref[:, theirs] = other(t_ref)


def place_kernel(plan, *refs):
    o_ref, sem = refs[-2:]
    me = lax.axis_index("cube")
    h = refs[0].shape[-1]
    copies = []
    for i, (array, index, level, source) in enumerate(plan):
        col = pl.multiple_of((me ^ source) * h, h)
        copies.append(
            pltpu.make_async_copy(refs[array].at[index], o_ref.at[level, :, pl.ds(col, h)], sem.at[i])
        )
    for copy in copies:
        copy.start()
    for copy in copies:
        copy.wait()


def place(run, blocks, plan, out, so_far=None):
    more = [] if so_far is None else [so_far]
    res = pl.pallas_call(
        functools.partial(place_kernel, plan),
        out_shape=out,
        in_specs=[pl.BlockSpec(memory_space=pl.ANY)] * (len(blocks) + len(more)),
        out_specs=pl.BlockSpec(memory_space=pl.ANY),
        scratch_shapes=[pltpu.SemaphoreType.DMA((len(plan),))],
        input_output_aliases={len(blocks): 0} if more else {},
        compiler_params=pltpu.CompilerParams(vmem_limit_bytes=1 << 20),
    )(after(blocks[0], run.last), *blocks[1:], *more)
    run.last = res
    return res


def local(rhs, dinv, own, far, cot, top, elem_map):
    levels, h, k = rhs.shape
    r, kh = 2 * h, k // 2
    n = lax.axis_size("cube")
    base = n.bit_length() - 1 - levels
    last = levels - 1
    run = Sequence()
    vec, vec_t, half_t, front = shape(r, kh), shape(kh, r), shape(kh, h), shape(r, r, dtype=BF16)

    top_t = swap(top)
    pf, d0 = run(
        functools.partial(take_kernel, last),
        [far, dinv],
        [shape(h, r)] * 2,
        [pltpu.SemaphoreType.DMA((2,))],
        hbm=(0, 1),
    )
    pf_t, d0_t = swap(pf), swap(d0)
    rhs_t, cot_t = swap(rhs), swap(cot)
    x = run.named(
        first_kernel,
        {"pf": pf, "pf_t": pf_t, "d0": d0, "d0_t": d0_t, "top": top, "top_t": top_t, "rhs": rhs, "rhs_t": rhs_t},
        {
            "s": vec, "y": vec_t, "w": vec_t, "wm": half_t, "wt": half_t, "rows": shape(levels, r, kh),
            "ph": front, "pl": front, "dh": front, "dl": front,
        },
    )
    raw = {"far": far, "own": own, "dinv": dinv}
    raw.update({name + "_t": swap(after(v, top_t, pf_t, d0_t, rhs_t, cot_t)) for name, v in raw.items()})
    parts = {f"far{last}h": x["ph"], f"far{last}l": x["pl"], "dinv0h": x["dh"], "dinv0l": x["dl"]}
    rows = x["rows"]
    s, st, wm, wt = ([None] * levels for _ in range(4))
    s[0], w, y, wm[last], wt[last] = x["s"], x["w"], x["y"], x["wm"], x["wt"]
    st[0] = swap(s[0])

    nears, fars = range(NEAR), range(n // NEAR)

    def outer(batch, by_near):
        one = shape(len(batch), len(fars if by_near else nears), r // n, h)
        return run(
            functools.partial(outer_kernel, len(batch), by_near),
            [elem_map, *(v for q in batch for v in (s[q], st[q], wm[q], wt[q]))],
            [one] * len(nears if by_near else fars),
            limit=12,
        )

    def exchange(arrays, step):
        return [
            arrays[0],
            *(lax.ppermute(v, "cube", [(i, i ^ j * step) for i in range(n)]) for j, v in enumerate(arrays) if j),
        ]

    def turn(arrays):
        batch, count, e, width = arrays[0].shape
        return run(
            functools.partial(turn_kernel, len(arrays)), arrays, [shape(batch, len(arrays), e, width)] * count
        )

    early, late = list(range(1, levels - 1)), [0, last]
    for t in range(levels):
        lf, lb = t, last - t
        yp = partner(y, base + lb)
        if t < last:
            sp = partner(s[lf], base + lf)
        if t == 0:
            new = [(name, q) for name in raw if "_t" not in name for q in range(levels)]
            new = [q for q in new if f"{q[0]}{q[1]}h" not in parts]
            parts.update(
                run.named(
                    functools.partial(prep_kernel, new),
                    {"far_t": raw["far_t"], "own_t": raw["own_t"], "dinv_t": raw["dinv_t"],
                     "far": far, "own": own, "dinv": dinv},
                    {f"{name}{level}{e}": front for name, level in new for e in "hl"},
                    scratch=[VMEM((len(new), h, r), F32), pltpu.SemaphoreType.DMA((len(new),))],
                    hbm=(3, 4, 5),
                )
            )
        x = run.named(
            functools.partial(own_kernel, lb),
            {
                "s": s[lf], "w": w, "cot": cot, "cot_t": cot_t,
                "ph": parts[f"own{lf}h"], "pl": parts[f"own{lf}l"],
                "qh": parts[f"own{lb}h"], "ql": parts[f"own{lb}l"],
            },
            {"a": vec, "b": vec_t},
        )
        a, b = x["a"], x["b"]
        if t == levels - 2:
            crossed = exchange(outer(early, False), NEAR)
        if t < last:
            x = run.named(
                bwd_next,
                {
                    "b": b, "yp": yp,
                    **{p + e: parts[f"{q}{e}"] for e in "hl" for p, q in (("d", f"dinv{lb}"), ("p", f"far{lb - 1}"))},
                },
                {"y": vec_t, "w": vec_t, "wm": half_t, "ws": half_t},
            )
            w, y, wm[lb - 1], wt[lb - 1] = x["w"], x["y"], x["wm"], (both if t == levels - 2 else swap)(x["ws"])
            x = run.named(
                functools.partial(fwd_next, t + 1),
                {
                    "a": a, "sp": sp, "rows": rows,
                    **{p + e: parts[f"{q}{e}"] for e in "hl" for p, q in (("p", f"far{lf}"), ("d", f"dinv{lf + 1}"))},
                },
                {"s": vec},
            )
            s[t + 1] = x["s"]
            st[t + 1] = (swap if t == 0 else both)(s[t + 1])
    late_out = exchange(outer(late, True), 1)
    early_in = exchange(turn(crossed), 1)
    late_in = exchange(turn(late_out), NEAR)
    sp = partner(after(s[last], *crossed), base + last)
    out = shape(levels, r // n, n * h)
    plan = [(m, (i, f), lv, m + NEAR * f) for m in nears for f in fars for i, lv in enumerate(early)]
    element_grad = place(run, early_in, plan, out)
    g = run.named(
        bwd_last,
        {"b": b, "yp": yp, "dh": parts["dinv0h"], "dl": parts["dinv0l"]},
        {"g": vec_t, "gm": half_t, "gs": half_t},
    )
    gms, gts = [g["gm"], *wm[:last]], [both(g["gs"]), *wt[:last]]
    solved, grads = run(
        results_kernel,
        [v for q in range(levels) for v in (s[q], st[q], gms[q], gts[q])],
        [shape(levels, h, k), shape(levels, h, k)],
    )
    u = run.named(
        fwd_last,
        {"a": a, "sp": sp, "ph": parts[f"far{last}h"], "pl": parts[f"far{last}l"]},
        {"u": vec, "um": shape(h, kh), "us": shape(h, kh)},
    )
    top_update, = run(join_kernel, [u["um"], both(u["us"])], [shape(h, k)])
    plan = [(f, (i, m), lv, m + NEAR * f) for m in nears for f in fars for i, lv in enumerate(late)]
    element_grad = place(run, late_in, plan, out, element_grad)
    return solved, top_update, grads, element_grad


def solution(mesh):
    rows = P(None, ("cube", "cores"), None)
    return jax.shard_map(
        local,
        mesh=mesh,
        in_specs=(rows, rows, rows, rows, rows, P(("cube", "cores"), None), P("cube", None)),
        out_specs=(rows, P(("cube", "cores"), None), rows, P(None, "cube", "cores")),
        check_vma=False,
    )
```

```python
import functools
import types

import jax
import jax.numpy as jnp
from jax import lax
from jax.experimental import pallas as pl
from jax.experimental.pallas import tpu as pltpu
from jax.sharding import PartitionSpec as P

F32, BF16 = jnp.float32, jnp.bfloat16
VMEM = pltpu.VMEM
NEAR = 4


def partner(x, distance):
    return lax.ppermute(x, "cube", [(i, i ^ 1 << distance) for i in range(lax.axis_size("cube"))])


def swap(x):
    return lax.ppermute(x, "cores", [(0, 1), (1, 0)])


def both(x):
    return lax.all_gather(x, "cores")


def other(ref):
    return ref[1 - lax.axis_index("cores")] if len(ref.shape) == 3 else ref[...]


def split(x):
    hi = x.astype(BF16)
    return hi, (x - hi.astype(F32)).astype(BF16)


def dot(a, b):
    return lax.dot_general(a, b, (((1,), (0,)), ((), ())), preferred_element_type=F32)


def mul(hi, lo, v):
    n = v.shape[1]
    vh, vl = split(v)
    t = dot(hi, jnp.concatenate([vh, vl], axis=1))
    return t[:, :n] + t[:, n:] + dot(lo, vh)


def mul_t(v, hi, lo):
    n = v.shape[0]
    vh, vl = split(v)
    t = dot(jnp.concatenate([vh, vl], axis=0), hi)
    return t[:n] + t[n:] + dot(vh, lo)


class Sequence:
    def __init__(self):
        self.last = None

    def __call__(self, kernel, args, outs, scratch=(), limit=8, hbm=()):
        args = list(args)
        if self.last is not None:
            args[0] = after(args[0], self.last)
        for i in hbm:
            args[i] = pltpu.with_memory_space_constraint(args[i], pltpu.HBM)
        res = pl.pallas_call(
            kernel,
            out_shape=tuple(outs),
            in_specs=[pl.BlockSpec(memory_space=pltpu.HBM if i in hbm else VMEM) for i in range(len(args))],
            out_specs=tuple(pl.BlockSpec(memory_space=VMEM) for _ in outs),
            scratch_shapes=list(scratch),
            compiler_params=pltpu.CompilerParams(vmem_limit_bytes=limit << 20),
        )(*args)
        self.last = res[-1]
        return res

    def named(self, kernel, args, outs, **more):
        def body(*refs):
            ins, rest = refs[: len(args)], refs[len(args) :]
            kernel(
                types.SimpleNamespace(**dict(zip(args, ins))),
                types.SimpleNamespace(**dict(zip(outs, rest))),
                *rest[len(outs) :],
            )

        return dict(zip(outs, self(body, args.values(), outs.values(), **more)))


def shape(*s, dtype=F32):
    return jax.ShapeDtypeStruct(s, dtype)


def after(x, *others):
    return lax.optimization_barrier((x, *others))[0]


def halves(h):
    c = lax.axis_index("cores")
    return pl.multiple_of(c * h, h), pl.multiple_of((1 - c) * h, h)


def whole(m_ref, t_ref, level, hi_ref, lo_ref):
    h = hi_ref.shape[0] // 2
    for ref, off in zip((m_ref, t_ref), halves(h)):
        hi, lo = split(ref[...] if level is None else ref[level])
        hi_ref[pl.ds(off, h), :] = hi
        lo_ref[pl.ds(off, h), :] = lo


def take_kernel(last, far_ref, dinv_ref, pf_ref, d0_ref, sem):
    copies = [
        pltpu.make_async_copy(far_ref.at[last], pf_ref, sem.at[0]),
        pltpu.make_async_copy(dinv_ref.at[0], d0_ref, sem.at[1]),
    ]
    for copy in copies:
        copy.start()
    for copy in copies:
        copy.wait()


def first_kernel(refs, outs):
    h, k = refs.top.shape[0], refs.top.shape[1] // 2
    mine, theirs = halves(k)
    row_mine, row_theirs = halves(h)
    whole(refs.pf, refs.pf_t, None, outs.ph, outs.pl)
    outs.wm[...] = refs.top[:, pl.ds(mine, k)].T
    outs.w[:, pl.ds(row_mine, h)] = outs.wm[...]
    outs.w[:, pl.ds(row_theirs, h)] = refs.top_t[:, pl.ds(mine, k)].T
    outs.y[...] = mul_t(outs.w[...], outs.ph[...], outs.pl[...])
    whole(refs.d0, refs.d0_t, None, outs.dh, outs.dl)
    for level in range(refs.rhs.shape[0]):
        outs.rows[level, pl.ds(row_mine, h), :] = refs.rhs[level, :, pl.ds(mine, k)]
        outs.rows[level, pl.ds(row_theirs, h), :] = refs.rhs_t[level, :, pl.ds(mine, k)]
    outs.s[...] = mul(outs.dh[...], outs.dl[...], outs.rows[0])
    outs.wt[...] = refs.top[:, pl.ds(theirs, k)].T


def prep_kernel(new, refs, outs, buf, sem):
    copies = [
        pltpu.make_async_copy(getattr(refs, name).at[level], buf.at[i], sem.at[i])
        for i, (name, level) in enumerate(new)
    ]
    for copy in copies:
        copy.start()
    for i, (name, level) in enumerate(new):
        copies[i].wait()
        hi, lo = getattr(outs, f"{name}{level}h"), getattr(outs, f"{name}{level}l")
        h = hi.shape[0] // 2
        mine, theirs = halves(h)
        for v, off in ((buf[i], mine), (getattr(refs, name + "_t")[level], theirs)):
            v_hi, v_lo = split(v)
            hi[pl.ds(off, h), :] = v_hi
            lo[pl.ds(off, h), :] = v_lo


def fwd_own(refs, outs):
    outs.a[...] = mul(refs.h[...], refs.l[...], refs.s[...])


def bwd_own(level, refs, outs):
    h, k = refs.cot.shape[1], refs.cot.shape[2] // 2
    mine, _ = halves(k)
    for ref, off in zip((refs.cot, refs.cot_t), halves(h)):
        outs.b[:, pl.ds(off, h)] = ref[level, :, pl.ds(mine, k)].T
    outs.b[...] += mul_t(refs.w[...], refs.h[...], refs.l[...])


def fwd_next(level, refs, outs):
    u = refs.a[...] + mul(refs.ph[...], refs.pl[...], refs.sp[...])
    outs.s[...] = mul(refs.dh[...], refs.dl[...], refs.rows[level] - u)


def bwd_next(refs, outs):
    outs.w[...] = -mul_t(refs.b[...] + refs.yp[...], refs.dh[...], refs.dl[...])
    outs.y[...] = mul_t(outs.w[...], refs.ph[...], refs.pl[...])
    h = outs.wm.shape[1]
    mine, theirs = halves(h)
    outs.wm[...] = outs.w[:, pl.ds(mine, h)]
    outs.ws[...] = outs.w[:, pl.ds(theirs, h)]


def bwd_last(refs, outs):
    w = refs.b[...] + refs.yp[...]
    outs.g[...] = -mul_t(w, refs.dh[...], refs.dl[...])
    h = outs.gm.shape[1]
    mine, theirs = halves(h)
    outs.gm[...] = outs.g[:, pl.ds(mine, h)]
    outs.gs[...] = outs.g[:, pl.ds(theirs, h)]


def fwd_last(refs, outs):
    outs.u[...] = refs.a[...] + mul(refs.ph[...], refs.pl[...], refs.sp[...])
    h = outs.um.shape[0]
    mine, theirs = halves(h)
    outs.um[...] = outs.u[pl.ds(mine, h), :]
    outs.us[...] = outs.u[pl.ds(theirs, h), :]


def outer_kernel(batch, by_near, map_ref, *refs):
    ins, outs = refs[: 4 * batch], refs[4 * batch :]
    r = ins[0].shape[0]
    e = outs[0].shape[2]
    target = map_ref[...] ^ (lax.axis_index("cube") * e)
    pick = jnp.where(lax.broadcasted_iota(jnp.int32, (r, r), 0) == target, 1.0, 0.0).astype(BF16)
    for i in range(batch):
        s_ref, st_ref, wm_ref, wt_ref = ins[4 * i : 4 * i + 4]
        sh, sl = split(jnp.concatenate([s_ref[...], other(st_ref)], axis=1))
        ph = dot(pick, sh).astype(BF16)
        plo = dot(pick, sl).astype(BF16)
        wh, wl = split(jnp.concatenate([wm_ref[...], other(wt_ref)], axis=0))
        o = dot(ph, wh) + dot(ph, wl) + dot(plo, wh)
        for j, out in enumerate(outs):
            for q in range(out.shape[1]):
                at = (j + NEAR * q if by_near else q + NEAR * j) * e
                out[i, q] = o[at : at + e]


def turn_kernel(n_in, *refs):
    ins, outs = refs[:n_in], refs[n_in:]
    for q, out in enumerate(outs):
        for j, ref in enumerate(ins):
            for i in range(ref.shape[0]):
                out[i, j] = ref[i, q]


def results_kernel(*refs):
    solved_ref, grad_ref = refs[-2:]
    levels, h, k = solved_ref.shape
    k //= 2
    mine, _ = halves(h)
    own, theirs = (pl.ds(x, k) for x in halves(k))
    for level in range(levels):
        s_ref, st_ref, gm_ref, gt_ref = refs[4 * level : 4 * level + 4]
        solved_ref[level, :, own] = s_ref[pl.ds(mine, h), :]
        st = st_ref if len(st_ref.shape) == 2 else st_ref.at[1 - lax.axis_index("cores")]
        solved_ref[level, :, theirs] = st[pl.ds(mine, h), :]
        grad_ref[level, :, own] = -gm_ref[...].T
        grad_ref[level, :, theirs] = -other(gt_ref).T


def join_kernel(m_ref, t_ref, o_ref):
    k = m_ref.shape[1]
    own, theirs = (pl.ds(x, k) for x in halves(k))
    o_ref[:, own] = m_ref[...]
    o_ref[:, theirs] = other(t_ref)


def place_kernel(plan, *refs):
    o_ref, sem = refs[-2:]
    me = lax.axis_index("cube")
    h = refs[0].shape[-1]
    copies = []
    for i, (array, index, level, source) in enumerate(plan):
        col = pl.multiple_of((me ^ source) * h, h)
        copies.append(
            pltpu.make_async_copy(refs[array].at[index], o_ref.at[level, :, pl.ds(col, h)], sem.at[i])
        )
    for copy in copies:
        copy.start()
    for copy in copies:
        copy.wait()


def place(run, blocks, plan, out, so_far=None):
    more = [] if so_far is None else [so_far]
    res = pl.pallas_call(
        functools.partial(place_kernel, plan),
        out_shape=out,
        in_specs=[pl.BlockSpec(memory_space=pl.ANY)] * (len(blocks) + len(more)),
        out_specs=pl.BlockSpec(memory_space=pl.ANY),
        scratch_shapes=[pltpu.SemaphoreType.DMA((len(plan),))],
        input_output_aliases={len(blocks): 0} if more else {},
        compiler_params=pltpu.CompilerParams(vmem_limit_bytes=1 << 20),
    )(after(blocks[0], run.last), *blocks[1:], *more)
    run.last = res
    return res


def local(rhs, dinv, own, far, cot, top, elem_map):
    levels, h, k = rhs.shape
    r, kh = 2 * h, k // 2
    n = lax.axis_size("cube")
    base = n.bit_length() - 1 - levels
    last = levels - 1
    run = Sequence()
    vec, vec_t, half_t, front = shape(r, kh), shape(kh, r), shape(kh, h), shape(r, r, dtype=BF16)

    top_t = swap(top)
    pf, d0 = run(
        functools.partial(take_kernel, last),
        [far, dinv],
        [shape(h, r)] * 2,
        [pltpu.SemaphoreType.DMA((2,))],
        hbm=(0, 1),
    )
    pf_t, d0_t = swap(pf), swap(d0)
    rhs_t, cot_t = swap(rhs), swap(cot)
    x = run.named(
        first_kernel,
        {"pf": pf, "pf_t": pf_t, "d0": d0, "d0_t": d0_t, "top": top, "top_t": top_t, "rhs": rhs, "rhs_t": rhs_t},
        {
            "s": vec, "y": vec_t, "w": vec_t, "wm": half_t, "wt": half_t, "rows": shape(levels, r, kh),
            "ph": front, "pl": front, "dh": front, "dl": front,
        },
    )
    raw = {"far": far, "own": own, "dinv": dinv}
    raw.update({name + "_t": swap(after(v, top_t, pf_t, d0_t, rhs_t, cot_t)) for name, v in raw.items()})
    parts = {f"far{last}h": x["ph"], f"far{last}l": x["pl"], "dinv0h": x["dh"], "dinv0l": x["dl"]}
    rows = x["rows"]
    s, st, wm, wt = ([None] * levels for _ in range(4))
    s[0], w, y, wm[last], wt[last] = x["s"], x["w"], x["y"], x["wm"], x["wt"]
    st[0] = swap(s[0])

    nears, fars = range(NEAR), range(n // NEAR)

    def outer(batch, by_near):
        one = shape(len(batch), len(fars if by_near else nears), r // n, h)
        return run(
            functools.partial(outer_kernel, len(batch), by_near),
            [elem_map, *(v for q in batch for v in (s[q], st[q], wm[q], wt[q]))],
            [one] * len(nears if by_near else fars),
            limit=12,
        )

    def exchange(arrays, step):
        return [
            arrays[0],
            *(lax.ppermute(v, "cube", [(i, i ^ j * step) for i in range(n)]) for j, v in enumerate(arrays) if j),
        ]

    def turn(arrays):
        batch, count, e, width = arrays[0].shape
        return run(
            functools.partial(turn_kernel, len(arrays)), arrays, [shape(batch, len(arrays), e, width)] * count
        )

    early, late = list(range(1, levels - 1)), [0, last]
    yp = partner(y, base + last)
    sp = partner(s[0], base)
    new = [(name, q) for name in raw if "_t" not in name for q in range(levels)]
    new = [q for q in new if f"{q[0]}{q[1]}h" not in parts]
    parts.update(
        run.named(
            functools.partial(prep_kernel, new),
            {
                "far_t": raw["far_t"], "own_t": raw["own_t"], "dinv_t": raw["dinv_t"],
                "far": far, "own": own, "dinv": dinv,
            },
            {f"{name}{level}{e}": front for name, level in new for e in "hl"},
            scratch=[VMEM((len(new), h, r), F32), pltpu.SemaphoreType.DMA((len(new),))],
            hbm=(3, 4, 5),
        )
    )

    def pick(**fronts):
        return {p + e: parts[f"{q}{e}"] for p, q in fronts.items() for e in "hl"}

    def own_a(t):
        fronts = {e: parts[f"own{t}{e}"] for e in "hl"}
        return run.named(fwd_own, {"s": s[t], **fronts}, {"a": vec})["a"]

    def own_b(t):
        fronts = {e: parts[f"own{t}{e}"] for e in "hl"}
        args = {"w": w, "cot": cot, "cot_t": cot_t, **fronts}
        return run.named(functools.partial(bwd_own, t), args, {"b": vec_t})["b"]

    for t in range(last):
        lb = last - t
        if t == last - 1:
            crossed = exchange(outer(early, False), NEAR)
        x = run.named(
            functools.partial(fwd_next, t + 1),
            {"a": own_a(t), "sp": sp, "rows": rows, **pick(p=f"far{t}", d=f"dinv{t + 1}")},
            {"s": vec},
        )
        s[t + 1] = x["s"]
        sp = partner(s[t + 1], base + t + 1)
        st[t + 1] = (both if t == last - 1 else swap)(s[t + 1])
        x = run.named(
            bwd_next,
            {"b": own_b(lb), "yp": yp, **pick(d=f"dinv{lb}", p=f"far{lb - 1}")},
            {"y": vec_t, "w": vec_t, "wm": half_t, "ws": half_t},
        )
        w, y, wm[lb - 1], wt[lb - 1] = x["w"], x["y"], x["wm"], (both if t == last - 1 else swap)(x["ws"])
        yp = partner(y, base + lb - 1)
    late_out = exchange(outer(late, True), 1)
    a = own_a(last)
    b = own_b(0)
    early_in = exchange(turn(crossed), 1)
    late_in = exchange(turn(late_out), NEAR)
    u = run.named(
        fwd_last,
        {"a": a, "sp": sp, "ph": parts[f"far{last}h"], "pl": parts[f"far{last}l"]},
        {"u": vec, "um": shape(h, kh), "us": shape(h, kh)},
    )
    out = shape(levels, r // n, n * h)
    plan = [(m, (i, f), lv, m + NEAR * f) for m in nears for f in fars for i, lv in enumerate(early)]
    element_grad = place(run, early_in, plan, out)
    g = run.named(
        bwd_last,
        {"b": b, "yp": yp, "dh": parts["dinv0h"], "dl": parts["dinv0l"]},
        {"g": vec_t, "gm": half_t, "gs": half_t},
    )
    gms, gts = [g["gm"], *wm[:last]], [both(g["gs"]), *wt[:last]]
    solved, grads = run(
        results_kernel,
        [v for q in range(levels) for v in (s[q], st[q], gms[q], gts[q])],
        [shape(levels, h, k), shape(levels, h, k)],
    )
    top_update, = run(join_kernel, [u["um"], both(u["us"])], [shape(h, k)])
    plan = [(f, (i, m), lv, m + NEAR * f) for m in nears for f in fars for i, lv in enumerate(late)]
    element_grad = place(run, late_in, plan, out, element_grad)
    return solved, top_update, grads, element_grad


def solution(mesh):
    rows = P(None, ("cube", "cores"), None)
    return jax.shard_map(
        local,
        mesh=mesh,
        in_specs=(rows, rows, rows, rows, rows, P(("cube", "cores"), None), P("cube", None)),
        out_specs=(rows, P(("cube", "cores"), None), rows, P(None, "cube", "cores")),
        check_vma=False,
    )
```

```python
import functools
import types

import jax
import jax.numpy as jnp
from jax import lax
from jax.experimental import pallas as pl
from jax.experimental.pallas import tpu as pltpu
from jax.sharding import PartitionSpec as P

F32, BF16 = jnp.float32, jnp.bfloat16
VMEM = pltpu.VMEM
NEAR = 4


def partner(x, distance):
    return lax.ppermute(x, "cube", [(i, i ^ 1 << distance) for i in range(lax.axis_size("cube"))])


def swap(x):
    return lax.ppermute(x, "cores", [(0, 1), (1, 0)])


def both(x):
    return lax.all_gather(x, "cores")


def other(ref):
    return ref[1 - lax.axis_index("cores")] if len(ref.shape) == 3 else ref[...]


def split(x):
    hi = x.astype(BF16)
    return hi, (x - hi.astype(F32)).astype(BF16)


def dot(a, b):
    return lax.dot_general(a, b, (((1,), (0,)), ((), ())), preferred_element_type=F32)


def mul(hi, lo, v):
    n = v.shape[1]
    vh, vl = split(v)
    t = dot(hi, jnp.concatenate([vh, vl], axis=1))
    return t[:, :n] + t[:, n:] + dot(lo, vh)


def mul_t(v, hi, lo):
    n = v.shape[0]
    vh, vl = split(v)
    t = dot(jnp.concatenate([vh, vl], axis=0), hi)
    return t[:n] + t[n:] + dot(vh, lo)


class Sequence:
    def __init__(self):
        self.last = None

    def __call__(self, kernel, args, outs, scratch=(), limit=8, hbm=()):
        args = list(args)
        if self.last is not None:
            args[0] = after(args[0], self.last)
        for i in hbm:
            args[i] = pltpu.with_memory_space_constraint(args[i], pltpu.HBM)
        res = pl.pallas_call(
            kernel,
            out_shape=tuple(outs),
            in_specs=[pl.BlockSpec(memory_space=pltpu.HBM if i in hbm else VMEM) for i in range(len(args))],
            out_specs=tuple(pl.BlockSpec(memory_space=VMEM) for _ in outs),
            scratch_shapes=list(scratch),
            compiler_params=pltpu.CompilerParams(vmem_limit_bytes=limit << 20),
        )(*args)
        self.last = res[-1]
        return res

    def named(self, kernel, args, outs, **more):
        def body(*refs):
            ins, rest = refs[: len(args)], refs[len(args) :]
            kernel(
                types.SimpleNamespace(**dict(zip(args, ins))),
                types.SimpleNamespace(**dict(zip(outs, rest))),
                *rest[len(outs) :],
            )

        return dict(zip(outs, self(body, args.values(), outs.values(), **more)))


def shape(*s, dtype=F32):
    return jax.ShapeDtypeStruct(s, dtype)


def after(x, *others):
    return lax.optimization_barrier((x, *others))[0]


def halves(h):
    c = lax.axis_index("cores")
    return pl.multiple_of(c * h, h), pl.multiple_of((1 - c) * h, h)


def whole(m_ref, t_ref, level, hi_ref, lo_ref):
    h = hi_ref.shape[0] // 2
    for ref, off in zip((m_ref, t_ref), halves(h)):
        hi, lo = split(ref[...] if level is None else ref[level])
        hi_ref[pl.ds(off, h), :] = hi
        lo_ref[pl.ds(off, h), :] = lo


def take_kernel(last, far_ref, dinv_ref, pf_ref, d0_ref, sem):
    copies = [
        pltpu.make_async_copy(far_ref.at[last], pf_ref, sem.at[0]),
        pltpu.make_async_copy(dinv_ref.at[0], d0_ref, sem.at[1]),
    ]
    for copy in copies:
        copy.start()
    for copy in copies:
        copy.wait()


def first_kernel(refs, outs):
    h, k = refs.top.shape[0], refs.top.shape[1] // 2
    mine, theirs = halves(k)
    row_mine, row_theirs = halves(h)
    whole(refs.pf, refs.pf_t, None, outs.ph, outs.pl)
    outs.wm[...] = refs.top[:, pl.ds(mine, k)].T
    outs.w[:, pl.ds(row_mine, h)] = outs.wm[...]
    outs.w[:, pl.ds(row_theirs, h)] = refs.top_t[:, pl.ds(mine, k)].T
    outs.y[...] = mul_t(outs.w[...], outs.ph[...], outs.pl[...])
    whole(refs.d0, refs.d0_t, None, outs.dh, outs.dl)
    for level in range(refs.rhs.shape[0]):
        outs.rows[level, pl.ds(row_mine, h), :] = refs.rhs[level, :, pl.ds(mine, k)]
        outs.rows[level, pl.ds(row_theirs, h), :] = refs.rhs_t[level, :, pl.ds(mine, k)]
    outs.s[...] = mul(outs.dh[...], outs.dl[...], outs.rows[0])
    outs.wt[...] = refs.top[:, pl.ds(theirs, k)].T


def prep_kernel(new, refs, outs, buf, sem):
    copies = [
        pltpu.make_async_copy(getattr(refs, name).at[level], buf.at[i], sem.at[i])
        for i, (name, level) in enumerate(new)
    ]
    for copy in copies:
        copy.start()
    for i, (name, level) in enumerate(new):
        copies[i].wait()
        hi, lo = getattr(outs, f"{name}{level}h"), getattr(outs, f"{name}{level}l")
        h = hi.shape[0] // 2
        mine, theirs = halves(h)
        for v, off in ((buf[i], mine), (getattr(refs, name + "_t")[level], theirs)):
            v_hi, v_lo = split(v)
            hi[pl.ds(off, h), :] = v_hi
            lo[pl.ds(off, h), :] = v_lo


def fwd_own(refs, outs):
    outs.a[...] = mul(refs.h[...], refs.l[...], refs.s[...])


def bwd_own(level, refs, outs):
    h, k = refs.cot.shape[1], refs.cot.shape[2] // 2
    mine, _ = halves(k)
    for ref, off in zip((refs.cot, refs.cot_t), halves(h)):
        outs.b[:, pl.ds(off, h)] = ref[level, :, pl.ds(mine, k)].T
    outs.b[...] += mul_t(refs.w[...], refs.h[...], refs.l[...])


def fwd_next(level, refs, outs):
    u = refs.a[...] + mul(refs.ph[...], refs.pl[...], refs.sp[...])
    outs.s[...] = mul(refs.dh[...], refs.dl[...], refs.rows[level] - u)


def bwd_next(refs, outs):
    outs.w[...] = -mul_t(refs.b[...] + refs.yp[...], refs.dh[...], refs.dl[...])
    outs.y[...] = mul_t(outs.w[...], refs.ph[...], refs.pl[...])
    h = outs.wm.shape[1]
    mine, theirs = halves(h)
    outs.wm[...] = outs.w[:, pl.ds(mine, h)]
    outs.ws[...] = outs.w[:, pl.ds(theirs, h)]


def bwd_last(refs, outs):
    w = refs.b[...] + refs.yp[...]
    outs.g[...] = -mul_t(w, refs.dh[...], refs.dl[...])
    h = outs.gm.shape[1]
    mine, theirs = halves(h)
    outs.gm[...] = outs.g[:, pl.ds(mine, h)]
    outs.gs[...] = outs.g[:, pl.ds(theirs, h)]


def fwd_last(refs, outs):
    outs.u[...] = refs.a[...] + mul(refs.ph[...], refs.pl[...], refs.sp[...])
    h = outs.um.shape[0]
    mine, theirs = halves(h)
    outs.um[...] = outs.u[pl.ds(mine, h), :]
    outs.us[...] = outs.u[pl.ds(theirs, h), :]


def outer_kernel(batch, by_near, map_ref, *refs):
    ins, outs = refs[: 4 * batch], refs[4 * batch :]
    r = ins[0].shape[0]
    e = outs[0].shape[2]
    target = map_ref[...] ^ (lax.axis_index("cube") * e)
    pick = jnp.where(lax.broadcasted_iota(jnp.int32, (r, r), 0) == target, 1.0, 0.0).astype(BF16)
    for i in range(batch):
        s_ref, st_ref, wm_ref, wt_ref = ins[4 * i : 4 * i + 4]
        sh, sl = split(jnp.concatenate([s_ref[...], other(st_ref)], axis=1))
        ph = dot(pick, sh).astype(BF16)
        plo = dot(pick, sl).astype(BF16)
        wh, wl = split(jnp.concatenate([wm_ref[...], other(wt_ref)], axis=0))
        o = dot(ph, wh) + dot(ph, wl) + dot(plo, wh)
        for j, out in enumerate(outs):
            for q in range(out.shape[1]):
                at = (j + NEAR * q if by_near else q + NEAR * j) * e
                out[i, q] = o[at : at + e]


def turn_kernel(n_in, *refs):
    ins, outs = refs[:n_in], refs[n_in:]
    for q, out in enumerate(outs):
        for j, ref in enumerate(ins):
            for i in range(ref.shape[0]):
                out[i, j] = ref[i, q]


def results_kernel(*refs):
    solved_ref, grad_ref = refs[-2:]
    levels, h, k = solved_ref.shape
    k //= 2
    mine, _ = halves(h)
    own, theirs = (pl.ds(x, k) for x in halves(k))
    for level in range(levels):
        s_ref, st_ref, gm_ref, gt_ref = refs[4 * level : 4 * level + 4]
        solved_ref[level, :, own] = s_ref[pl.ds(mine, h), :]
        st = st_ref if len(st_ref.shape) == 2 else st_ref.at[1 - lax.axis_index("cores")]
        solved_ref[level, :, theirs] = st[pl.ds(mine, h), :]
        grad_ref[level, :, own] = -gm_ref[...].T
        grad_ref[level, :, theirs] = -other(gt_ref).T


def join_kernel(m_ref, t_ref, o_ref):
    k = m_ref.shape[1]
    own, theirs = (pl.ds(x, k) for x in halves(k))
    o_ref[:, own] = m_ref[...]
    o_ref[:, theirs] = other(t_ref)


def place_kernel(plan, *refs):
    o_ref, sem = refs[-2:]
    me = lax.axis_index("cube")
    h = refs[0].shape[-1]
    copies = []
    for i, (array, index, level, source) in enumerate(plan):
        col = pl.multiple_of((me ^ source) * h, h)
        copies.append(
            pltpu.make_async_copy(refs[array].at[index], o_ref.at[level, :, pl.ds(col, h)], sem.at[i])
        )
    for copy in copies:
        copy.start()
    for copy in copies:
        copy.wait()


def place(run, blocks, plan, out, so_far=None):
    more = [] if so_far is None else [so_far]
    res = pl.pallas_call(
        functools.partial(place_kernel, plan),
        out_shape=out,
        in_specs=[pl.BlockSpec(memory_space=pl.ANY)] * (len(blocks) + len(more)),
        out_specs=pl.BlockSpec(memory_space=pl.ANY),
        scratch_shapes=[pltpu.SemaphoreType.DMA((len(plan),))],
        input_output_aliases={len(blocks): 0} if more else {},
        compiler_params=pltpu.CompilerParams(vmem_limit_bytes=1 << 20),
    )(after(blocks[0], run.last), *blocks[1:], *more)
    run.last = res
    return res


def local(rhs, dinv, own, far, cot, top, elem_map):
    levels, h, k = rhs.shape
    r, kh = 2 * h, k // 2
    n = lax.axis_size("cube")
    base = n.bit_length() - 1 - levels
    last = levels - 1
    run = Sequence()
    vec, vec_t, half_t, front = shape(r, kh), shape(kh, r), shape(kh, h), shape(r, r, dtype=BF16)

    top_t = swap(top)
    pf, d0 = run(
        functools.partial(take_kernel, last),
        [far, dinv],
        [shape(h, r)] * 2,
        [pltpu.SemaphoreType.DMA((2,))],
        hbm=(0, 1),
    )
    pf_t, d0_t = swap(pf), swap(d0)
    rhs_t, cot_t = swap(rhs), swap(cot)
    x = run.named(
        first_kernel,
        {"pf": pf, "pf_t": pf_t, "d0": d0, "d0_t": d0_t, "top": top, "top_t": top_t, "rhs": rhs, "rhs_t": rhs_t},
        {
            "s": vec, "y": vec_t, "w": vec_t, "wm": half_t, "wt": half_t, "rows": shape(levels, r, kh),
            "ph": front, "pl": front, "dh": front, "dl": front,
        },
    )
    raw = {"far": far, "own": own, "dinv": dinv}
    raw.update({name + "_t": swap(after(v, top_t, pf_t, d0_t, rhs_t, cot_t)) for name, v in raw.items()})
    parts = {f"far{last}h": x["ph"], f"far{last}l": x["pl"], "dinv0h": x["dh"], "dinv0l": x["dl"]}
    rows = x["rows"]
    s, st, wm, wt = ([None] * levels for _ in range(4))
    s[0], w, y, wm[last], wt[last] = x["s"], x["w"], x["y"], x["wm"], x["wt"]
    st[0] = swap(s[0])

    nears, fars = range(NEAR), range(n // NEAR)

    def outer(batch, by_near):
        one = shape(len(batch), len(fars if by_near else nears), r // n, h)
        return run(
            functools.partial(outer_kernel, len(batch), by_near),
            [elem_map, *(v for q in batch for v in (s[q], st[q], wm[q], wt[q]))],
            [one] * len(nears if by_near else fars),
            limit=12,
        )

    def exchange(arrays, step):
        return [
            arrays[0],
            *(lax.ppermute(v, "cube", [(i, i ^ j * step) for i in range(n)]) for j, v in enumerate(arrays) if j),
        ]

    def turn(arrays):
        batch, count, e, width = arrays[0].shape
        return run(
            functools.partial(turn_kernel, len(arrays)), arrays, [shape(batch, len(arrays), e, width)] * count
        )

    early, late = list(range(1, levels - 1)), [0, last]
    yp = partner(y, base + last)
    sp = partner(s[0], base)
    new = [(name, q) for name in raw if "_t" not in name for q in range(levels)]
    new = [q for q in new if f"{q[0]}{q[1]}h" not in parts]
    parts.update(
        run.named(
            functools.partial(prep_kernel, new),
            {
                "far_t": raw["far_t"], "own_t": raw["own_t"], "dinv_t": raw["dinv_t"],
                "far": far, "own": own, "dinv": dinv,
            },
            {f"{name}{level}{e}": front for name, level in new for e in "hl"},
            scratch=[VMEM((len(new), h, r), F32), pltpu.SemaphoreType.DMA((len(new),))],
            hbm=(3, 4, 5),
        )
    )

    def pick(**fronts):
        return {p + e: parts[f"{q}{e}"] for p, q in fronts.items() for e in "hl"}

    def own_a(t):
        fronts = {e: parts[f"own{t}{e}"] for e in "hl"}
        return run.named(fwd_own, {"s": s[t], **fronts}, {"a": vec})["a"]

    def own_b(t):
        fronts = {e: parts[f"own{t}{e}"] for e in "hl"}
        args = {"w": w, "cot": cot, "cot_t": cot_t, **fronts}
        return run.named(functools.partial(bwd_own, t), args, {"b": vec_t})["b"]

    for t in range(last):
        lb = last - t
        if t == last - 1:
            crossed = exchange(outer(early, False), NEAR)
        x = run.named(
            functools.partial(fwd_next, t + 1),
            {"a": own_a(t), "sp": sp, "rows": rows, **pick(p=f"far{t}", d=f"dinv{t + 1}")},
            {"s": vec},
        )
        s[t + 1] = x["s"]
        sp = partner(s[t + 1], base + t + 1)
        st[t + 1] = (both if t == last - 1 else swap)(s[t + 1])
        x = run.named(
            bwd_next,
            {"b": own_b(lb), "yp": yp, **pick(d=f"dinv{lb}", p=f"far{lb - 1}")},
            {"y": vec_t, "w": vec_t, "wm": half_t, "ws": half_t},
        )
        w, y, wm[lb - 1], wt[lb - 1] = x["w"], x["y"], x["wm"], (both if t == last - 1 else swap)(x["ws"])
        yp = partner(y, base + lb - 1)
    late_out = exchange(outer(late, True), 1)
    a = own_a(last)
    b = own_b(0)
    early_in = exchange(turn(crossed), 1)
    late_in = exchange(turn(late_out), NEAR)
    u = run.named(
        fwd_last,
        {"a": a, "sp": sp, "ph": parts[f"far{last}h"], "pl": parts[f"far{last}l"]},
        {"u": vec, "um": shape(h, kh), "us": shape(h, kh)},
    )
    out = shape(levels, r // n, n * h)
    plan = [(m, (i, f), lv, m + NEAR * f) for m in nears for f in fars for i, lv in enumerate(early)]
    element_grad = place(run, early_in, plan, out)
    g = run.named(
        bwd_last,
        {"b": b, "yp": yp, "dh": parts["dinv0h"], "dl": parts["dinv0l"]},
        {"g": vec_t, "gm": half_t, "gs": half_t},
    )
    gms, gts = [g["gm"], *wm[:last]], [both(g["gs"]), *wt[:last]]
    solved, grads = run(
        results_kernel,
        [v for q in range(levels) for v in (s[q], st[q], gms[q], gts[q])],
        [shape(levels, h, k), shape(levels, h, k)],
    )
    top_update, = run(join_kernel, [u["um"], both(u["us"])], [shape(h, k)])
    for part in (fars[: len(fars) // 2], fars[len(fars) // 2 :]):
        plan = [
            (f - part[0], (i, m), lv, m + NEAR * f) for m in nears for f in part for i, lv in enumerate(late)
        ]
        element_grad = place(run, [late_in[f] for f in part], plan, out, element_grad)
    return solved, top_update, grads, element_grad


def solution(mesh):
    rows = P(None, ("cube", "cores"), None)
    return jax.shard_map(
        local,
        mesh=mesh,
        in_specs=(rows, rows, rows, rows, rows, P(("cube", "cores"), None), P("cube", None)),
        out_specs=(rows, P(("cube", "cores"), None), rows, P(None, "cube", "cores")),
        check_vma=False,
    )
```

```python
import functools
import types

import jax
import jax.numpy as jnp
from jax import lax
from jax.experimental import pallas as pl
from jax.experimental.pallas import tpu as pltpu
from jax.sharding import PartitionSpec as P

F32, BF16 = jnp.float32, jnp.bfloat16
VMEM = pltpu.VMEM
NEAR = 4


def partner(x, distance):
    return lax.ppermute(x, "cube", [(i, i ^ 1 << distance) for i in range(lax.axis_size("cube"))])


def swap(x):
    return lax.ppermute(x, "cores", [(0, 1), (1, 0)])


def both(x):
    return lax.all_gather(x, "cores")


def other(ref):
    return ref[1 - lax.axis_index("cores")] if len(ref.shape) == 3 else ref[...]


def split(x):
    hi = x.astype(BF16)
    return hi, (x - hi.astype(F32)).astype(BF16)


def dot(a, b):
    return lax.dot_general(a, b, (((1,), (0,)), ((), ())), preferred_element_type=F32)


def mul(hi, lo, v):
    n = v.shape[1]
    vh, vl = split(v)
    t = dot(hi, jnp.concatenate([vh, vl], axis=1))
    return t[:, :n] + t[:, n:] + dot(lo, vh)


def mul_t(v, hi, lo):
    n = v.shape[0]
    vh, vl = split(v)
    t = dot(jnp.concatenate([vh, vl], axis=0), hi)
    return t[:n] + t[n:] + dot(vh, lo)


class Sequence:
    def __init__(self):
        self.last = None

    def __call__(self, kernel, args, outs, scratch=(), limit=8, hbm=()):
        args = list(args)
        if self.last is not None:
            args[0] = after(args[0], self.last)
        for i in hbm:
            args[i] = pltpu.with_memory_space_constraint(args[i], pltpu.HBM)
        res = pl.pallas_call(
            kernel,
            out_shape=tuple(outs),
            in_specs=[pl.BlockSpec(memory_space=pltpu.HBM if i in hbm else VMEM) for i in range(len(args))],
            out_specs=tuple(pl.BlockSpec(memory_space=VMEM) for _ in outs),
            scratch_shapes=list(scratch),
            compiler_params=pltpu.CompilerParams(vmem_limit_bytes=limit << 20),
        )(*args)
        self.last = res[-1]
        return res

    def named(self, kernel, args, outs, **more):
        def body(*refs):
            ins, rest = refs[: len(args)], refs[len(args) :]
            kernel(
                types.SimpleNamespace(**dict(zip(args, ins))),
                types.SimpleNamespace(**dict(zip(outs, rest))),
                *rest[len(outs) :],
            )

        return dict(zip(outs, self(body, args.values(), outs.values(), **more)))


def shape(*s, dtype=F32):
    return jax.ShapeDtypeStruct(s, dtype)


def after(x, *others):
    return lax.optimization_barrier((x, *others))[0]


def halves(h):
    c = lax.axis_index("cores")
    return pl.multiple_of(c * h, h), pl.multiple_of((1 - c) * h, h)


def whole(m_ref, t_ref, level, hi_ref, lo_ref):
    h = hi_ref.shape[0] // 2
    for ref, off in zip((m_ref, t_ref), halves(h)):
        hi, lo = split(ref[...] if level is None else ref[level])
        hi_ref[pl.ds(off, h), :] = hi
        lo_ref[pl.ds(off, h), :] = lo


def take_kernel(last, far_ref, dinv_ref, pf_ref, d0_ref, sem):
    copies = [
        pltpu.make_async_copy(far_ref.at[last], pf_ref, sem.at[0]),
        pltpu.make_async_copy(dinv_ref.at[0], d0_ref, sem.at[1]),
    ]
    for copy in copies:
        copy.start()
    for copy in copies:
        copy.wait()


def first_kernel(refs, outs):
    h, k = refs.top.shape[0], refs.top.shape[1] // 2
    mine, theirs = halves(k)
    row_mine, row_theirs = halves(h)
    whole(refs.pf, refs.pf_t, None, outs.ph, outs.pl)
    outs.wm[...] = refs.top[:, pl.ds(mine, k)].T
    outs.w[:, pl.ds(row_mine, h)] = outs.wm[...]
    outs.w[:, pl.ds(row_theirs, h)] = refs.top_t[:, pl.ds(mine, k)].T
    outs.y[...] = mul_t(outs.w[...], outs.ph[...], outs.pl[...])
    whole(refs.d0, refs.d0_t, None, outs.dh, outs.dl)
    for level in range(refs.rhs.shape[0]):
        outs.rows[level, pl.ds(row_mine, h), :] = refs.rhs[level, :, pl.ds(mine, k)]
        outs.rows[level, pl.ds(row_theirs, h), :] = refs.rhs_t[level, :, pl.ds(mine, k)]
    outs.s[...] = mul(outs.dh[...], outs.dl[...], outs.rows[0])
    outs.wt[...] = refs.top[:, pl.ds(theirs, k)].T


def prep_kernel(new, refs, outs, buf, sem):
    copies = [
        pltpu.make_async_copy(getattr(refs, name).at[level], buf.at[i], sem.at[i])
        for i, (name, level) in enumerate(new)
    ]
    for copy in copies:
        copy.start()
    for i, (name, level) in enumerate(new):
        copies[i].wait()
        hi, lo = getattr(outs, f"{name}{level}h"), getattr(outs, f"{name}{level}l")
        h = hi.shape[0] // 2
        mine, theirs = halves(h)
        for v, off in ((buf[i], mine), (getattr(refs, name + "_t")[level], theirs)):
            v_hi, v_lo = split(v)
            hi[pl.ds(off, h), :] = v_hi
            lo[pl.ds(off, h), :] = v_lo


def fwd_own(refs, outs):
    outs.a[...] = mul(refs.h[...], refs.l[...], refs.s[...])


def bwd_own(level, refs, outs):
    h, k = refs.cot.shape[1], refs.cot.shape[2] // 2
    mine, _ = halves(k)
    for ref, off in zip((refs.cot, refs.cot_t), halves(h)):
        outs.b[:, pl.ds(off, h)] = ref[level, :, pl.ds(mine, k)].T
    outs.b[...] += mul_t(refs.w[...], refs.h[...], refs.l[...])


def fwd_next(level, refs, outs):
    u = refs.a[...] + mul(refs.ph[...], refs.pl[...], refs.sp[...])
    outs.s[...] = mul(refs.dh[...], refs.dl[...], refs.rows[level] - u)


def bwd_next(refs, outs):
    outs.w[...] = -mul_t(refs.b[...] + refs.yp[...], refs.dh[...], refs.dl[...])
    outs.y[...] = mul_t(outs.w[...], refs.ph[...], refs.pl[...])
    h = outs.wm.shape[1]
    mine, theirs = halves(h)
    outs.wm[...] = outs.w[:, pl.ds(mine, h)]
    outs.ws[...] = outs.w[:, pl.ds(theirs, h)]


def bwd_last(refs, outs):
    w = refs.b[...] + refs.yp[...]
    outs.g[...] = -mul_t(w, refs.dh[...], refs.dl[...])
    h = outs.gm.shape[1]
    mine, theirs = halves(h)
    outs.gm[...] = outs.g[:, pl.ds(mine, h)]
    outs.gs[...] = outs.g[:, pl.ds(theirs, h)]


def fwd_last(refs, outs):
    outs.u[...] = refs.a[...] + mul(refs.ph[...], refs.pl[...], refs.sp[...])
    h = outs.um.shape[0]
    mine, theirs = halves(h)
    outs.um[...] = outs.u[pl.ds(mine, h), :]
    outs.us[...] = outs.u[pl.ds(theirs, h), :]


def outer_kernel(batch, by_near, map_ref, *refs):
    ins, outs = refs[: 4 * batch], refs[4 * batch :]
    r = ins[0].shape[0]
    e = outs[0].shape[2]
    target = map_ref[...] ^ (lax.axis_index("cube") * e)
    pick = jnp.where(lax.broadcasted_iota(jnp.int32, (r, r), 0) == target, 1.0, 0.0).astype(BF16)
    for i in range(batch):
        s_ref, st_ref, wm_ref, wt_ref = ins[4 * i : 4 * i + 4]
        sh, sl = split(jnp.concatenate([s_ref[...], other(st_ref)], axis=1))
        ph = dot(pick, sh).astype(BF16)
        plo = dot(pick, sl).astype(BF16)
        wh, wl = split(jnp.concatenate([wm_ref[...], other(wt_ref)], axis=0))
        o = dot(ph, wh) + dot(ph, wl) + dot(plo, wh)
        for j, out in enumerate(outs):
            for q in range(out.shape[1]):
                at = (j + NEAR * q if by_near else q + NEAR * j) * e
                out[i, q] = o[at : at + e]


def turn_kernel(n_in, *refs):
    ins, outs = refs[:n_in], refs[n_in:]
    for q, out in enumerate(outs):
        for j, ref in enumerate(ins):
            for i in range(ref.shape[0]):
                out[i, j] = ref[i, q]


def results_kernel(*refs):
    solved_ref, grad_ref = refs[-2:]
    levels, h, k = solved_ref.shape
    k //= 2
    mine, _ = halves(h)
    own, theirs = (pl.ds(x, k) for x in halves(k))
    for level in range(levels):
        s_ref, st_ref, gm_ref, gt_ref = refs[4 * level : 4 * level + 4]
        solved_ref[level, :, own] = s_ref[pl.ds(mine, h), :]
        st = st_ref if len(st_ref.shape) == 2 else st_ref.at[1 - lax.axis_index("cores")]
        solved_ref[level, :, theirs] = st[pl.ds(mine, h), :]
        grad_ref[level, :, own] = -gm_ref[...].T
        grad_ref[level, :, theirs] = -other(gt_ref).T


def join_kernel(m_ref, t_ref, o_ref):
    k = m_ref.shape[1]
    own, theirs = (pl.ds(x, k) for x in halves(k))
    o_ref[:, own] = m_ref[...]
    o_ref[:, theirs] = other(t_ref)


def place_kernel(plan, *refs):
    o_ref, sem = refs[-2:]
    me = lax.axis_index("cube")
    h = refs[0].shape[-1]
    copies = []
    for i, (array, index, level, source) in enumerate(plan):
        col = pl.multiple_of((me ^ source) * h, h)
        copies.append(
            pltpu.make_async_copy(refs[array].at[index], o_ref.at[level, :, pl.ds(col, h)], sem.at[i])
        )
    for copy in copies:
        copy.start()
    for copy in copies:
        copy.wait()


def place(run, blocks, plan, out, so_far=None):
    more = [] if so_far is None else [so_far]
    res = pl.pallas_call(
        functools.partial(place_kernel, plan),
        out_shape=out,
        in_specs=[pl.BlockSpec(memory_space=pl.ANY)] * (len(blocks) + len(more)),
        out_specs=pl.BlockSpec(memory_space=pl.ANY),
        scratch_shapes=[pltpu.SemaphoreType.DMA((len(plan),))],
        input_output_aliases={len(blocks): 0} if more else {},
        compiler_params=pltpu.CompilerParams(vmem_limit_bytes=1 << 20),
    )(after(blocks[0], run.last), *blocks[1:], *more)
    run.last = res
    return res


def local(rhs, dinv, own, far, cot, top, elem_map):
    levels, h, k = rhs.shape
    r, kh = 2 * h, k // 2
    n = lax.axis_size("cube")
    base = n.bit_length() - 1 - levels
    last = levels - 1
    run = Sequence()
    vec, vec_t, half_t, front = shape(r, kh), shape(kh, r), shape(kh, h), shape(r, r, dtype=BF16)

    top_t = swap(top)
    pf, d0 = run(
        functools.partial(take_kernel, last),
        [far, dinv],
        [shape(h, r)] * 2,
        [pltpu.SemaphoreType.DMA((2,))],
        hbm=(0, 1),
    )
    pf_t, d0_t = swap(pf), swap(d0)
    rhs_t, cot_t = swap(rhs), swap(cot)
    x = run.named(
        first_kernel,
        {"pf": pf, "pf_t": pf_t, "d0": d0, "d0_t": d0_t, "top": top, "top_t": top_t, "rhs": rhs, "rhs_t": rhs_t},
        {
            "s": vec, "y": vec_t, "w": vec_t, "wm": half_t, "wt": half_t, "rows": shape(levels, r, kh),
            "ph": front, "pl": front, "dh": front, "dl": front,
        },
    )
    raw = {"far": far, "own": own, "dinv": dinv}
    raw.update({name + "_t": swap(after(v, top_t, pf_t, d0_t, rhs_t, cot_t)) for name, v in raw.items()})
    parts = {f"far{last}h": x["ph"], f"far{last}l": x["pl"], "dinv0h": x["dh"], "dinv0l": x["dl"]}
    rows = x["rows"]
    s, st, wm, wt = ([None] * levels for _ in range(4))
    s[0], w, y, wm[last], wt[last] = x["s"], x["w"], x["y"], x["wm"], x["wt"]
    st[0] = swap(s[0])

    nears, fars = range(NEAR), range(n // NEAR)

    def outer(batch, by_near):
        one = shape(len(batch), len(fars if by_near else nears), r // n, h)
        return run(
            functools.partial(outer_kernel, len(batch), by_near),
            [elem_map, *(v for q in batch for v in (s[q], st[q], wm[q], wt[q]))],
            [one] * len(nears if by_near else fars),
            limit=12,
        )

    def exchange(arrays, step):
        return [
            arrays[0],
            *(lax.ppermute(v, "cube", [(i, i ^ j * step) for i in range(n)]) for j, v in enumerate(arrays) if j),
        ]

    def turn(arrays):
        batch, count, e, width = arrays[0].shape
        return run(
            functools.partial(turn_kernel, len(arrays)), arrays, [shape(batch, len(arrays), e, width)] * count
        )

    early, late = list(range(1, levels - 1)), [0, last]
    yp = partner(y, base + last)
    sp = partner(s[0], base)
    new = [(name, q) for name in raw if "_t" not in name for q in range(levels)]
    new = [q for q in new if f"{q[0]}{q[1]}h" not in parts]
    parts.update(
        run.named(
            functools.partial(prep_kernel, new),
            {
                "far_t": raw["far_t"], "own_t": raw["own_t"], "dinv_t": raw["dinv_t"],
                "far": far, "own": own, "dinv": dinv,
            },
            {f"{name}{level}{e}": front for name, level in new for e in "hl"},
            scratch=[VMEM((len(new), h, r), F32), pltpu.SemaphoreType.DMA((len(new),))],
            hbm=(3, 4, 5),
        )
    )

    def pick(**fronts):
        return {p + e: parts[f"{q}{e}"] for p, q in fronts.items() for e in "hl"}

    def own_a(t):
        fronts = {e: parts[f"own{t}{e}"] for e in "hl"}
        mine = after(s[t], st[0]) if t == 1 else s[t]
        return run.named(fwd_own, {"s": mine, **fronts}, {"a": vec})["a"]

    def own_b(t):
        fronts = {e: parts[f"own{t}{e}"] for e in "hl"}
        args = {"w": w, "cot": cot, "cot_t": cot_t, **fronts}
        return run.named(functools.partial(bwd_own, t), args, {"b": vec_t})["b"]

    for t in range(last):
        lb = last - t
        if t == last - 1:
            crossed = exchange(outer(early, False), NEAR)
        x = run.named(
            functools.partial(fwd_next, t + 1),
            {"a": own_a(t), "sp": sp, "rows": rows, **pick(p=f"far{t}", d=f"dinv{t + 1}")},
            {"s": vec},
        )
        s[t + 1] = x["s"]
        sp = partner(s[t + 1], base + t + 1)
        st[t + 1] = (both if t == last - 1 else swap)(s[t + 1])
        x = run.named(
            bwd_next,
            {"b": own_b(lb), "yp": yp, **pick(d=f"dinv{lb}", p=f"far{lb - 1}")},
            {"y": vec_t, "w": vec_t, "wm": half_t, "ws": half_t},
        )
        w, y, wm[lb - 1], wt[lb - 1] = x["w"], x["y"], x["wm"], (both if t == last - 1 else swap)(x["ws"])
        yp = partner(y, base + lb - 1)
    late_out = exchange(outer(late, True), 1)
    a = own_a(last)
    b = own_b(0)
    early_in = exchange(turn(crossed), 1)
    late_in = exchange(turn(late_out), NEAR)
    u = run.named(
        fwd_last,
        {"a": a, "sp": sp, "ph": parts[f"far{last}h"], "pl": parts[f"far{last}l"]},
        {"u": vec, "um": shape(h, kh), "us": shape(h, kh)},
    )
    out = shape(levels, r // n, n * h)
    plan = [(m, (i, f), lv, m + NEAR * f) for m in nears for f in fars for i, lv in enumerate(early)]
    element_grad = place(run, early_in, plan, out)
    g = run.named(
        bwd_last,
        {"b": b, "yp": yp, "dh": parts["dinv0h"], "dl": parts["dinv0l"]},
        {"g": vec_t, "gm": half_t, "gs": half_t},
    )
    gms, gts = [g["gm"], *wm[:last]], [both(g["gs"]), *wt[:last]]
    solved, grads = run(
        results_kernel,
        [v for q in range(levels) for v in (s[q], st[q], gms[q], gts[q])],
        [shape(levels, h, k), shape(levels, h, k)],
    )
    top_update, = run(join_kernel, [u["um"], both(u["us"])], [shape(h, k)])
    for part in (fars[: len(fars) // 2], fars[len(fars) // 2 :]):
        plan = [
            (f - part[0], (i, m), lv, m + NEAR * f) for m in nears for f in part for i, lv in enumerate(late)
        ]
        element_grad = place(run, [late_in[f] for f in part], plan, out, element_grad)
    return solved, top_update, grads, element_grad


def solution(mesh):
    rows = P(None, ("cube", "cores"), None)
    return jax.shard_map(
        local,
        mesh=mesh,
        in_specs=(rows, rows, rows, rows, rows, P(("cube", "cores"), None), P("cube", None)),
        out_specs=(rows, P(("cube", "cores"), None), rows, P(None, "cube", "cores")),
        check_vma=False,
    )
```
